256 devices in a mesh: tm: 16 (over y, x_hi, core), group: 16 (over z, x_lo).
Axes of the slice: x: 4 (x_hi: 2, x_lo: 2; x = x_hi * 2 + x_lo), y: 4, z: 8, core: 2. Of those that a mesh axis runs over, the one named last changes fastest.
Arguments:
- clips: bfloat16 [16, 128, 128, 512], P('group', 'tm'), may hold values from -6 to 6
- lengths: int32 [16, 8], P('group'), may hold values from 1 to 32, 128 in all within a row
- w_time: bfloat16 [3, 512, 512], P(None, 'tm'), may hold values from -0.15625 to 0.15625
- w_down: bfloat16 [3, 512, 512], P(None, 'tm'), may hold values from -0.15625 to 0.15625
- cotangent: bfloat16 [16, 64, 128, 512], P('group', 'tm'), may hold values from -6 to 6
Outputs:
- reduced: bfloat16 [16, 64, 128, 512], P('group', 'tm')
- grad_clips: bfloat16 [16, 128, 128, 512], P('group', 'tm')
- grad_time: float32 [3, 512, 512], P(None, 'tm')
- grad_down: float32 [3, 512, 512], P(None, 'tm')
The draws below stay inside these ranges and needn't reach their ends.
All inputs are finite; a program needn't handle non-finite values.
Results may differ from the reference program's by a relative error of at most 0.0052.
Values may be sent and summed in bfloat16 or wider, within the bound.
A program may use at most 64 MiB of HBM per device.

```python
import math
import jax
import jax.numpy as jnp
import numpy as np
from jax import lax

C = 512
S = 128
FD = 8
NC = 8
KT = 3
FR = 128
HALF = 64
GROUPS = 16
N_TM = 16


def raised(values, own_key, source, target, blocks, factor):
    def block_of(axis_at):
        return (jnp.arange(values.shape[axis_at]) // (values.shape[axis_at] // blocks)).reshape((-1,) + (1,) * (values.ndim - 1 - axis_at))

    first = jax.random.permutation(own_key, blocks)[block_of(target)]
    other_side = (block_of(target) + blocks // 2) % blocks
    return jnp.where((block_of(source) == first) | (block_of(source) == other_side), factor * values, values)


def shard_levels(rng, dims, pieces, least, high):
    level = 1.0
    for axis_at, blocks in pieces:
        heights = jax.random.uniform(jax.random.fold_in(jax.random.fold_in(rng, 6), axis_at), (blocks,), jnp.float32, least / len(pieces), high / len(pieces))
        level = level * jnp.repeat(jnp.exp(heights), dims[axis_at] // blocks).reshape((-1,) + (1,) * (len(dims) - 1 - axis_at))
    return level


def length_profile(amount, total, limit, skew):
    portions = [(1 << 20) // math.isqrt(rank ** skew) + 1 for rank in range(2, amount + 1)]
    surplus, holding = total - limit - (amount - 1), [1] * (amount - 1)
    while surplus > 0:
        movable = [i for i in range(amount - 1) if holding[i] < limit]
        pool, budget = sum([portions[i] for i in movable]), surplus
        for i in movable:
            addition = min(limit - holding[i], max(1, budget * portions[i] // pool), surplus)
            holding[i] = holding[i] + addition
            surplus = surplus - addition
    return np.array([limit] + holding)


def ragged(own_key, count, total, bound, slope):
    if count == 2:
        one = jax.random.randint(own_key, (), max(1, total - bound), min(bound, total - 1) + 1)
        return jnp.stack([one, total - one])
    sizes = jnp.asarray(length_profile(count, total, bound, slope), jnp.int32)
    couples = (count - 1) // 2
    source_of, sink = sizes[1:1 + 2 * couples:2], sizes[2:2 + 2 * couples:2]
    room = jnp.minimum(source_of - 1, bound - sink)
    shifted = jax.random.randint(jax.random.fold_in(own_key, 1), (couples,), 0, 1 << 20) % (room + 1)
    sizes = sizes.at[1:1 + 2 * couples:2].set(source_of - shifted).at[2:2 + 2 * couples:2].set(sink + shifted)
    return sizes[jax.random.permutation(jax.random.fold_in(own_key, 2), count)]


def bell_draw(own_key, shape, scale, limit, shards=(), kind=jnp.bfloat16):
    result = jax.random.normal(own_key, shape, jnp.float32) * scale
    if len(shards) > 0:
        result = shard_levels(own_key, shape, shards, -0.22, 0.18) * result
    return jnp.clip(result, min=-limit, max=limit).astype(kind)


def bell_draw_with(rng, shape, scale, bound, pieces, heavy, held_as=jnp.bfloat16):
    entries = scale * jax.random.normal(rng, shape, jnp.float32)
    if pieces:
        entries = entries * shard_levels(rng, shape, pieces, -0.22, 0.18)
    return jnp.clip(raised(entries, jax.random.fold_in(rng, 3), *heavy), -bound, bound).astype(held_as)


def setup_inputs(seed: int = 0) -> dict:
    arg_keys = jax.random.split(jax.random.key(seed), 6)
    return {
        "clips": bell_draw_with(arg_keys[0], (GROUPS, FR, S, C), 1.0, 6.0, ((0, 16), (1, 16)), (1, 3, 16, 2.0)),
        "lengths": jax.vmap(lambda own: ragged(own, NC, FD * N_TM, FD * N_TM // 4, 2))(jax.random.split(arg_keys[1], GROUPS)).reshape((GROUPS, NC)).astype(jnp.int32),
        "w_time": bell_draw(arg_keys[2], (KT, C, C), (3 * C) ** -0.5, 0.15625, ((1, 16),)),
        "w_down": bell_draw(arg_keys[3], (KT, C, C), (3 * C) ** -0.5, 0.15625, ((1, 16),)),
        "cotangent": bell_draw(arg_keys[4], (GROUPS, HALF, S, C), 1.0, 6.0, ((0, 16), (1, 16))),
    }


def clip_start(lengths_row, frames):
    ends = jnp.cumsum(lengths_row)
    return lax.optimization_barrier(jnp.sum(jnp.where(ends[None, :] <= frames[:, None], lengths_row[None, :], 0), axis=1)).astype(jnp.int32)

def features(x_wide):
    scale = lax.rsqrt(lax.optimization_barrier(jnp.mean(x_wide * x_wide, axis=-1, keepdims=True)) + 1e-06)
    return jax.nn.silu(x_wide * scale)

def project(block, weight):
    shape = block.shape
    flat = jnp.dot(block.reshape(-1, shape[-1]), weight, preferred_element_type=jnp.float32)
    return flat.reshape(shape[:-1] + (weight.shape[1],))

def outer(left, right):
    width = left.shape[-1]
    return jnp.dot(left.reshape(-1, width).T, right.reshape(-1, right.shape[-1]), preferred_element_type=jnp.float32)

def one_group(x_bf, lengths_row, cot, w_time, w_down):
    frame_count = x_bf.shape[0]
    half_count = frame_count // 2
    frames = jnp.arange(frame_count, dtype=jnp.int32)
    starts = clip_start(lengths_row, frames)
    x_wide = x_bf.astype(jnp.float32)
    h_in = features(x_wide).astype(jnp.bfloat16)
    zero_rim = jnp.zeros((2,) + h_in.shape[1:], jnp.bfloat16)
    h_ext = jnp.concatenate([zero_rim, h_in], axis=0)
    mixed = x_wide
    time_taps = []
    for offset in range(3):
        valid = frames - offset >= starts
        tapped = jnp.where(valid[:, None, None], h_ext[2 - offset:2 - offset + frame_count], jnp.zeros((), jnp.bfloat16))
        time_taps.append(tapped)
        mixed = mixed + project(tapped, w_time[offset])
    hidden = mixed.astype(jnp.bfloat16)
    out_frames = 2 * jnp.arange(half_count, dtype=jnp.int32)
    out_starts = clip_start(lengths_row, out_frames)
    hidden_ext = jnp.concatenate([zero_rim, hidden], axis=0)
    reduced = jnp.zeros((half_count,) + hidden.shape[1:], jnp.float32)
    down_taps = []
    for offset in range(3):
        valid = out_frames - offset >= out_starts
        tapped = jnp.where(valid[:, None, None], hidden_ext[2 - offset:2 - offset + frame_count][::2], jnp.zeros((), jnp.bfloat16))
        down_taps.append(tapped)
        reduced = reduced + project(tapped, w_down[offset])
    grad_down = jnp.stack([outer(down_taps[offset], cot) for offset in range(3)])
    grad_hidden = jnp.zeros(x_wide.shape, jnp.float32)
    for offset in range(3):
        valid = out_frames - offset >= out_starts
        spread = jnp.where(valid[:, None, None], project(cot, w_down[offset].T), jnp.zeros((), jnp.float32))
        placed = jnp.stack([spread, jnp.zeros_like(spread)], axis=1).reshape((frame_count,) + spread.shape[1:])
        placed = jnp.concatenate([placed, jnp.zeros((2,) + spread.shape[1:], jnp.float32)], axis=0)
        grad_hidden = grad_hidden + placed[offset:offset + frame_count]
    grad_mixed = grad_hidden.astype(jnp.bfloat16)
    grad_time = jnp.stack([outer(time_taps[offset], grad_mixed) for offset in range(3)])
    grad_ext = jnp.concatenate([grad_mixed, zero_rim], axis=0)
    grad_hin = jnp.zeros(x_wide.shape, jnp.float32)
    for offset in range(3):
        valid = frames >= clip_start(lengths_row, frames + offset)
        tapped = jnp.where(valid[:, None, None], grad_ext[offset:offset + frame_count], jnp.zeros((), jnp.bfloat16))
        grad_hin = grad_hin + project(tapped, w_time[offset].T)
    _, pullback = jax.vjp(features, x_wide)
    grad_feat = pullback(grad_hin)[0]
    grad_clips = (grad_hidden + grad_feat).astype(jnp.bfloat16)
    return (reduced.astype(jnp.bfloat16), grad_clips, grad_time, grad_down)

def reference(clips, lengths, w_time, w_down, cotangent):

    def step(carry, items):
        x_bf, lengths_row, cot = items
        reduced, grad_clips, grad_time, grad_down = one_group(x_bf, lengths_row, cot, w_time, w_down)
        return ((carry[0] + grad_time, carry[1] + grad_down), (reduced, grad_clips))
    start_sums = (jnp.zeros(w_time.shape, jnp.float32), jnp.zeros(w_down.shape, jnp.float32))
    sums, stacked = lax.scan(step, start_sums, (clips, lengths, cotangent))
    return (stacked[0], stacked[1], sums[0], sums[1])
```

```python
import functools

import jax
import jax.numpy as jnp
from jax import lax
from jax.experimental import pallas as pl
from jax.experimental.pallas import tpu as pltpu
from jax.sharding import PartitionSpec as P

MESH = pl.DeviceIdType.MESH
BF = jnp.bfloat16
F32 = jnp.float32
FD, HD, S, C, NC = 8, 4, 128, 512, 8
NT = 16
NZ = 8
EPS = 1e-06


def dot(a, b, ca, cb):
    return lax.dot_general(a, b, (((ca,), (cb,)), ((), ())), preferred_element_type=F32)


def device(x, y, z, core):
    return {"tm": y * 4 + (x // 2) * 2 + core, "group": z * 2 + x % 2}


def kernel(
    lengths,
    clips,
    wt_own,
    wd_own,
    cot,
    reduced,
    grad_clips,
    pieces,
    wt,
    wd,
    clips_halo,
    cot_ext,
    h_ext,
    taps,
    gh,
    gm,
    hid,
    dtaps,
    gtap,
    stage,
    acc,
    core_out,
    core_in,
    out1,
    in1,
    out2,
    in2,
    out3,
    in3,
    out4,
    in4,
    z_out,
    z_in,
    piece,
    w_send,
    w_recv,
    halo_send,
    halo_recv,
    core_send,
    core_recv,
    ring_send,
    ring_recv,
    z_send,
    z_recv,
    p_send,
    p_recv,
    l_sem,
):
    t = lax.axis_index("tm")
    group = lax.axis_index("group")
    y, xh, c = t // 4, (t // 2) % 2, t % 2
    z, xl = group // 2, group % 2
    x = 2 * xh + xl

    def at(dx, dy, dz, dc):
        return device((x + dx + 4) % 4, (y + dy + 4) % 4, (z + dz + NZ) % NZ, (c + dc) % 2)

    sibling = at(0, 0, 0, 1)
    up, down = at(0, 1, 0, 0), at(0, -1, 0, 0)
    mirror = device(3 - x, y, z, c)
    step = 2 * c - 1
    far = {"tm": (t + step + NT) % NT, "group": group}

    def remote(src, dst, send, recv, target):
        return pltpu.make_async_remote_copy(
            src_ref=src,
            dst_ref=dst,
            send_sem=send,
            recv_sem=recv,
            device_id=target,
            device_id_type=MESH,
        )

    barrier = pltpu.get_barrier_semaphore()
    peers = [sibling, up, down, at(1, 0, 0, 0), at(-1, 0, 0, 0), far]
    peers += [at(0, 0, d, 0) for d in range(1, NZ)]
    mate = 1 - 2 * xl
    peers += [at(mate, 0, d, 0) for d in range(1, NZ)]
    for peer in peers:
        pl.semaphore_signal(barrier, inc=1, device_id=peer, device_id_type=MESH)
    pl.semaphore_wait(barrier, len(peers))

    def clips_copy(target):
        return remote(
            clips.at[pl.ds(FD - 4, 4)], clips_halo, halo_send.at[0], halo_recv.at[0], target
        )

    def cot_copy(target):
        return remote(
            cot.at[pl.ds(0, 2)], cot_ext.at[pl.ds(HD, 2)], halo_send.at[1], halo_recv.at[1], target
        )

    after = {"tm": (t + 1) % NT, "group": group}
    before = {"tm": (t + NT - 1) % NT, "group": group}

    def rows(ref, owner):
        return ref.at[:, pl.ds(pl.multiple_of(owner * 32, 32), 32), :]

    def owner_of(dy, other):
        h = 1 - xh if other else xh
        return ((y + dy + 4) % 4) * 4 + h * 2 + c

    blocks = [(0, 1), (-1, 0), (1, 0), (-1, 1), (1, 1), (2, 0), (2, 1)]

    def block_send(w, number, src, owner, to, slot):
        full = (wd, wt)[w]
        return remote(
            rows(full, owner) if src is None else src,
            rows(full, owner),
            w_send.at[w, number],
            w_recv.at[w, slot],
            to,
        )

    def first_sends(w):
        own = (wd_own, wt_own)[w]
        return [
            block_send(w, 0, own, t, up, 1),
            block_send(w, 1, own, t, down, 2),
            block_send(w, 2, own, t, mirror, 0),
            block_send(w, 3, own, t, sibling, 7),
        ]

    def passes(w, index):
        owner = owner_of(*blocks[index])
        sends = [block_send(w, 4 + index, None, owner, sibling, 8 + index)]
        if index == 0:
            sends = [
                block_send(w, 11, None, owner, up, 3),
                block_send(w, 12, None, owner, down, 4),
            ] + sends
        if index == 1:
            sends = [block_send(w, 13, None, owner, up, 5)] + sends
        if index == 4:
            sends = [block_send(w, 14, None, owner, down, 6)] + sends
        return sends

    def own_copy(w):
        return pltpu.make_async_copy(
            (wd_own, wt_own)[w], rows((wd, wt)[w], t), l_sem.at[w]
        )

    def arrive(w, index):
        owner = owner_of(*blocks[index])
        block_send(w, 4 + index, None, owner, sibling, index).wait_recv()
        for copy in passes(w, index):
            copy.start()

    def finish_weights(w):
        own_copy(w).wait()
        full = (wd, wt)[w]
        for slot in range(7, 15):
            other = t + 1 - 2 * c if slot == 7 else owner_of(*blocks[slot - 8]) + 1 - 2 * c
            block_send(w, 0, None, other, sibling, slot).wait_recv()

    for copy in first_sends(0):
        copy.start()
    own_copy(0).start()
    own_copy(1).start()

    @pl.when(t > 0)
    def _():
        cot_copy(before).start()

    @pl.when(t < NT - 1)
    def _():
        clips_copy(after).start()

    def length(i):
        return lengths[0, i]

    ends = [length(0)]
    for i in range(1, NC):
        ends.append(ends[-1] + length(i))
    first = t * FD

    def opens(frame):
        f = first + frame
        hit = f == 0
        for end in ends:
            hit = jnp.logical_or(hit, f == end)
        return hit

    opening = {i: opens(i) for i in range(-3, 11)}

    def live(k, frame):
        if k == 0:
            return None
        out = jnp.logical_not(opening[frame])
        if k == 2:
            out = jnp.logical_and(out, jnp.logical_not(opening[frame - 1]))
        return out

    def masked(keep, value):
        return value if keep is None else jnp.where(keep, value, jnp.zeros_like(value))

    def features(block):
        wide = block.astype(F32)
        scale = lax.rsqrt(jnp.mean(wide * wide, axis=-1, keepdims=True) + EPS)
        v = wide * scale
        return (v / (1.0 + jnp.exp(-v))).astype(BF)

    def feature_body(i, _):
        h_ext[4 + i] = features(clips[i])
        return 0

    cot_ext[pl.ds(0, HD)] = cot[...]
    lax.fori_loop(0, FD // 2, feature_body, 0)
    arrive(0, 0)
    lax.fori_loop(FD // 2, FD, feature_body, 0)
    arrive(0, 1)
    arrive(0, 2)
    for copy in first_sends(1):
        copy.start()
    arrive(0, 3)
    arrive(0, 4)
    arrive(0, 5)
    arrive(0, 6)

    @pl.when(t < NT - 1)
    def _():
        cot_copy(before).wait_recv()

    @pl.when(t == NT - 1)
    def _():
        cot_ext[pl.ds(HD, 2)] = jnp.zeros((2, S, C), BF)

    finish_weights(0)

    flat0 = cot_ext[pl.ds(0, 5)].reshape(5 * S, C)
    flat1 = cot_ext[pl.ds(1, 5)].reshape(5 * S, C)
    p0 = dot(flat0, wd[0], 1, 1).reshape(5, S, C)
    for j in range(5):
        gh[2 * j] = p0[j]
    p2 = dot(flat1, wd[2], 1, 1).reshape(5, S, C)
    for j in range(5):
        total = gh[2 * j] + masked(live(2, 2 * j + 2), p2[j])
        gh[2 * j] = total
        gm[2 * j] = total.astype(BF)
    p1 = dot(flat1, wd[1], 1, 1).reshape(5, S, C)
    for j in range(5):
        total = masked(live(1, 2 * j + 2), p1[j])
        gh[2 * j + 1] = total
        gm[2 * j + 1] = total.astype(BF)

    arrive(1, 0)
    arrive(1, 1)
    arrive(1, 2)

    @pl.when(t > 0)
    def _():
        clips_copy(after).wait_recv()

    @pl.when(t == 0)
    def _():
        clips_halo[...] = jnp.zeros((4, S, C), BF)

    def halo_body(i, _):
        h_ext[i] = features(clips_halo[i])
        return 0

    lax.fori_loop(0, 4, halo_body, 0)
    for k in range(3):
        for i in range(10):
            taps[k, i] = masked(live(k, i - 2), h_ext[i + 2 - k])

    def core_copy(g, k):
        return remote(
            core_out.at[g, k], core_in.at[g, k], core_send.at[g, k], core_recv.at[g, k], sibling
        )

    def contribute(g, k, value):
        stage[g] = value.reshape(4, 2, 2, 2, 16, C)
        for yy in range(4):
            for h in range(2):
                for l in range(2):
                    acc[g, k, 2 * h + l, yy] = stage[g, yy, h, c, l]
                    core_out[g, k, 2 * h + l, yy] = stage[g, yy, h, 1 - c, l].astype(BF)
        core_copy(g, k).start()

    def merge(g):
        for k in range(3):
            core_copy(g, k).wait_recv()
            acc[g, k] = acc[g, k] + core_in[g, k].astype(F32)

    def neighbours(along_x):
        if along_x:
            return x, at(1, 0, 0, 0), at(-1, 0, 0, 0)
        return y, up, down

    def outer_block(g, index):
        return acc.at[g, :, index] if g == 0 else acc.at[g, :, :, index]

    def inner_block(g, index):
        return acc.at[g, :, x, index] if g == 0 else acc.at[g, :, index, y]

    def ring_copy(g, stage_no, side, target):
        src = (out1, out2, out3, out4)[stage_no].at[g, side]
        dst = (in1, in2, in3, in4)[stage_no].at[g, side]
        return remote(
            src,
            dst,
            ring_send.at[g, stage_no, side],
            ring_recv.at[g, stage_no, side],
            target,
        )

    def ring_recv_wait(g, stage_no, side, target):
        ring_copy(g, stage_no, side, target).wait_recv()

    def outer1(g):
        at_, plus, minus = neighbours(g == 0)
        block = outer_block(g, (at_ + 2) % 4)
        out1[g, 0] = block[:, pl.ds(0, 2)].astype(BF)
        ring_copy(g, 0, 0, plus).start()
        out1[g, 1] = block[:, pl.ds(2, 2)].astype(BF)
        ring_copy(g, 0, 1, minus).start()

    def outer2(g):
        at_, plus, minus = neighbours(g == 0)
        block = outer_block(g, (at_ + 1) % 4)
        ring_recv_wait(g, 0, 0, plus)
        out2[g, 0, :, pl.ds(0, 2)] = (block[:, pl.ds(0, 2)] + in1[g, 0].astype(F32)).astype(BF)
        out2[g, 0, :, pl.ds(2, 2)] = block[:, pl.ds(2, 2)].astype(BF)
        ring_copy(g, 1, 0, plus).start()
        block = outer_block(g, (at_ + 3) % 4)
        ring_recv_wait(g, 0, 1, minus)
        out2[g, 1, :, pl.ds(2, 2)] = (block[:, pl.ds(2, 2)] + in1[g, 1].astype(F32)).astype(BF)
        out2[g, 1, :, pl.ds(0, 2)] = block[:, pl.ds(0, 2)].astype(BF)
        ring_copy(g, 1, 1, minus).start()

    def outer3(g):
        at_, plus, minus = neighbours(g == 0)
        ring_recv_wait(g, 1, 0, plus)
        ring_recv_wait(g, 1, 1, minus)
        block = outer_block(g, at_)
        block[...] = block[...] + in2[g, 0].astype(F32) + in2[g, 1].astype(F32)

    def inner1(g):
        at_, plus, minus = neighbours(g == 1)
        block = inner_block(g, (at_ + 2) % 4)
        out3[g, 0] = block[:, :, pl.ds(0, 256)].astype(BF)
        ring_copy(g, 2, 0, plus).start()
        out3[g, 1] = block[:, :, pl.ds(256, 256)].astype(BF)
        ring_copy(g, 2, 1, minus).start()

    def inner2(g):
        at_, plus, minus = neighbours(g == 1)
        block = inner_block(g, (at_ + 1) % 4)
        ring_recv_wait(g, 2, 0, plus)
        out4[g, 0, :, :, pl.ds(0, 256)] = (
            block[:, :, pl.ds(0, 256)] + in3[g, 0].astype(F32)
        ).astype(BF)
        out4[g, 0, :, :, pl.ds(256, 256)] = block[:, :, pl.ds(256, 256)].astype(BF)
        ring_copy(g, 3, 0, plus).start()
        block = inner_block(g, (at_ + 3) % 4)
        ring_recv_wait(g, 2, 1, minus)
        out4[g, 1, :, :, pl.ds(256, 256)] = (
            block[:, :, pl.ds(256, 256)] + in3[g, 1].astype(F32)
        ).astype(BF)
        out4[g, 1, :, :, pl.ds(0, 256)] = block[:, :, pl.ds(0, 256)].astype(BF)
        ring_copy(g, 3, 1, minus).start()

    def inner3(g):
        at_, plus, minus = neighbours(g == 1)
        ring_recv_wait(g, 3, 0, plus)
        ring_recv_wait(g, 3, 1, minus)
        block = acc.at[g, :, x, y]
        block[...] = block[...] + in4[g, 0].astype(F32) + in4[g, 1].astype(F32)

    def time_grad(k):
        left = taps[k, pl.ds(2, FD)].reshape(FD * S, C)
        contribute(0, k, dot(left, gm[pl.ds(0, FD)].reshape(FD * S, C), 0, 0))

    time_grad(0)
    arrive(1, 3)
    arrive(1, 4)
    time_grad(1)
    arrive(1, 5)
    arrive(1, 6)
    time_grad(2)
    for k in range(1, 3):
        for f in range(FD):
            gtap[k - 1, f] = masked(live(k, f + k), gm[f + k])
    finish_weights(1)

    def hidden_pair(i, wide):
        total = wide
        for k in range(3):
            total = total + dot(taps[k, pl.ds(i, 2)].reshape(2 * S, C), wt[k], 1, 0)
        hid[pl.ds(i, 2)] = total.astype(BF).reshape(2, S, C)

    hidden_pair(0, clips_halo[pl.ds(2, 2)].astype(F32).reshape(2 * S, C))

    def hidden_body(i, _):
        hidden_pair(2 + 2 * i, clips[pl.ds(2 * i, 2)].astype(F32).reshape(2 * S, C))
        return 0

    lax.fori_loop(0, FD // 2, hidden_body, 0)
    merge(0)
    outer1(0)
    for k in range(3):
        for j in range(HD):
            dtaps[k, j] = masked(live(k, 2 * j), hid[2 * j + 2 - k])

    def down_grad(k):
        contribute(1, k, dot(dtaps[k].reshape(HD * S, C), cot[...].reshape(HD * S, C), 0, 0))

    down_grad(0)
    down_grad(1)
    down_grad(2)
    outer2(0)
    total = dot(dtaps[0].reshape(HD * S, C), wd[0], 1, 0)
    total = total + dot(dtaps[1].reshape(HD * S, C), wd[1], 1, 0)
    total = total + dot(dtaps[2].reshape(HD * S, C), wd[2], 1, 0)
    reduced[...] = total.astype(BF).reshape(HD, S, C)
    merge(1)
    outer1(1)

    def clips_pair(i, _):
        here = pl.ds(2 * i, 2)
        g = dot(gm[here].reshape(2 * S, C), wt[0], 1, 1)
        g = g + dot(gtap[0, here].reshape(2 * S, C), wt[1], 1, 1)
        g = g + dot(gtap[1, here].reshape(2 * S, C), wt[2], 1, 1)
        wide = clips[here].astype(F32).reshape(2 * S, C)
        scale = lax.rsqrt(jnp.mean(wide * wide, axis=-1, keepdims=True) + EPS)
        v = wide * scale
        sig = 1.0 / (1.0 + jnp.exp(-v))
        d = g * (sig * (1.0 + v * (1.0 - sig)))
        inner = jnp.mean(d * v, axis=-1, keepdims=True)
        grad = (d - v * inner) * scale
        grad_clips[here] = (gh[here].reshape(2 * S, C) + grad).astype(BF).reshape(2, S, C)
        return 0

    lax.fori_loop(0, 1, clips_pair, 0)
    outer3(0)
    inner1(0)
    lax.fori_loop(1, 2, clips_pair, 0)
    outer2(1)
    lax.fori_loop(2, 3, clips_pair, 0)
    inner2(0)
    lax.fori_loop(3, 4, clips_pair, 0)
    inner3(0)
    outer3(1)
    inner1(1)
    inner2(1)
    inner3(1)

    def z_copy(d):
        return remote(
            z_out.at[d - 1], z_in.at[d - 1], z_send.at[d - 1], z_recv.at[d - 1], at(0, 0, d, 0)
        )

    for g in range(2):
        for q in range(4):
            z_out[8 + g * 4 + q] = acc[g, :, x, y, :, pl.ds(128 * q, 128)].astype(BF)
    for d in range(1, NZ):
        z_out[d - 1] = z_out[8 + (z + d) % NZ]
        z_copy(d).start()
    total = z_out[8 + z].astype(F32)
    for d in range(1, NZ):
        z_copy(d).wait_recv()
        total = total + z_in[d - 1].astype(F32)
    piece[...] = total.astype(BF)

    def piece_copy(other, d):
        number = other * NZ + d - 1
        return remote(
            piece, pieces.at[z, xl], p_send.at[number], p_recv.at[number], at(mate * other, 0, d, 0)
        )

    sends = [(1, d) for d in range(NZ)] + [(0, d) for d in range(1, NZ)]
    for other, d in sends:
        piece_copy(other, d).start()
    pieces[z, xl] = piece[...]
    for other, d in sends:
        piece_copy(other, d).wait()

    @pl.when(t > 0)
    def _():
        cot_copy(before).wait_send()

    @pl.when(t < NT - 1)
    def _():
        clips_copy(after).wait_send()

    for w in range(2):
        for copy in first_sends(w):
            copy.wait_send()
        for index in range(7):
            for copy in passes(w, index):
                copy.wait_send()
    for g in range(2):
        for k in range(3):
            core_copy(g, k).wait_send()
        for stage_no in range(4):
            _, plus, minus = neighbours((g == 0) == (stage_no < 2))
            ring_copy(g, stage_no, 0, plus).wait_send()
            ring_copy(g, stage_no, 1, minus).wait_send()
    for d in range(1, NZ):
        z_copy(d).wait_send()


def shards(clips, lengths, w_time, w_down, cotangent):
    vmem = pl.BlockSpec(memory_space=pltpu.VMEM)
    dma = pltpu.SemaphoreType.DMA
    reduced, grad_clips, pieces = pl.pallas_call(
        kernel,
        out_shape=(
            jax.ShapeDtypeStruct((HD, S, C), BF),
            jax.ShapeDtypeStruct((FD, S, C), BF),
            jax.ShapeDtypeStruct((NZ, 2, 3, 16, 128), BF),
        ),
        in_specs=[pl.BlockSpec(memory_space=pltpu.SMEM)] + [vmem] * 4,
        out_specs=(vmem, vmem, vmem),
        scratch_shapes=[
            pltpu.VMEM((3, C, C), BF),
            pltpu.VMEM((3, C, C), BF),
            pltpu.VMEM((4, S, C), BF),
            pltpu.VMEM((HD + 2, S, C), BF),
            pltpu.VMEM((FD + 4, S, C), BF),
            pltpu.VMEM((3, FD + 2, S, C), BF),
            pltpu.VMEM((FD + 2, S, C), F32),
            pltpu.VMEM((FD + 2, S, C), BF),
            pltpu.VMEM((FD + 2, S, C), BF),
            pltpu.VMEM((3, HD, S, C), BF),
            pltpu.VMEM((2, FD, S, C), BF),
            pltpu.VMEM((2, 4, 2, 2, 2, 16, C), F32),
            pltpu.VMEM((2, 3, 4, 4, 16, C), F32),
            pltpu.VMEM((2, 3, 4, 4, 16, C), BF),
            pltpu.VMEM((2, 3, 4, 4, 16, C), BF),
            pltpu.VMEM((2, 2, 3, 2, 16, C), BF),
            pltpu.VMEM((2, 2, 3, 2, 16, C), BF),
            pltpu.VMEM((2, 2, 3, 4, 16, C), BF),
            pltpu.VMEM((2, 2, 3, 4, 16, C), BF),
            pltpu.VMEM((2, 2, 3, 16, 256), BF),
            pltpu.VMEM((2, 2, 3, 16, 256), BF),
            pltpu.VMEM((2, 2, 3, 16, C), BF),
            pltpu.VMEM((2, 2, 3, 16, C), BF),
            pltpu.VMEM((2 * NZ, 3, 16, 128), BF),
            pltpu.VMEM((NZ - 1, 3, 16, 128), BF),
            pltpu.VMEM((3, 16, 128), BF),
            dma((2, 15)),
            dma((2, 15)),
            dma((2,)),
            dma((2,)),
            dma((2, 3)),
            dma((2, 3)),
            dma((2, 4, 2)),
            dma((2, 4, 2)),
            dma((NZ - 1,)),
            dma((NZ - 1,)),
            dma((2 * NZ,)),
            dma((2 * NZ,)),
            dma((2,)),
        ],
        name="clip_conv",
        compiler_params=pltpu.CompilerParams(
            collective_id=0, has_side_effects=True, vmem_limit_bytes=60 * 2**20
        ),
    )(lengths, clips[0], w_time, w_down, cotangent[0])
    grads = pieces.reshape(2, 4, 2, 3, 16, 128).transpose(0, 3, 2, 4, 1, 5)
    grads = grads.reshape(2, 3, 32, C).astype(F32)
    return reduced[None], grad_clips[None], grads[0], grads[1]


def solution(mesh):
    in_specs = (
        P("group", "tm", None, None),
        P("group", None),
        P(None, "tm", None),
        P(None, "tm", None),
        P("group", "tm", None, None),
    )
    out_specs = (
        P("group", "tm", None, None),
        P("group", "tm", None, None),
        P(None, "tm", None),
        P(None, "tm", None),
    )
    return jax.shard_map(shards, mesh=mesh, in_specs=in_specs, out_specs=out_specs, check_vma=False)
```

```python
import functools

import jax
import jax.numpy as jnp
from jax import lax
from jax.experimental import pallas as pl
from jax.experimental.pallas import tpu as pltpu
from jax.sharding import PartitionSpec as P

MESH = pl.DeviceIdType.MESH
BF = jnp.bfloat16
F32 = jnp.float32
FD, HD, S, C, NC = 8, 4, 128, 512, 8
NT = 16
NZ = 8
EPS = 1e-06


def dot(a, b, ca, cb):
    return lax.dot_general(a, b, (((ca,), (cb,)), ((), ())), preferred_element_type=F32)


def device(x, y, z, core):
    return {"tm": y * 4 + (x // 2) * 2 + core, "group": z * 2 + x % 2}


def kernel(
    lengths,
    clips_in,
    wt_own,
    wd_own,
    cot_in,
    reduced_out,
    clips_out,
    pieces,
    clips,
    reduced,
    grad_clips,
    wt,
    wd,
    clips_halo,
    cot_ext,
    h_ext,
    taps,
    gh,
    gm,
    hid,
    dtaps,
    gtap,
    stage,
    acc,
    core_out,
    core_in,
    outer_out,
    outer_in,
    inner_out,
    inner_in,
    z_wide,
    z_out,
    z_in,
    piece,
    w_send,
    w_recv,
    halo_send,
    halo_recv,
    core_send,
    core_recv,
    outer_send,
    outer_recv,
    inner_send,
    inner_recv,
    z_send,
    z_recv,
    p_send,
    p_recv,
    l_sem,
):
    t = lax.axis_index("tm")
    group = lax.axis_index("group")
    y, xh, c = t // 4, (t // 2) % 2, t % 2
    z, xl = group // 2, group % 2
    x = 2 * xh + xl

    def at(dx, dy, dz, dc):
        return device((x + dx + 4) % 4, (y + dy + 4) % 4, (z + dz + NZ) % NZ, (c + dc) % 2)

    sibling = at(0, 0, 0, 1)
    up, down = at(0, 1, 0, 0), at(0, -1, 0, 0)
    mirror = device(3 - x, y, z, c)
    step = 2 * c - 1
    far = {"tm": (t + step + NT) % NT, "group": group}

    def remote(src, dst, send, recv, target):
        return pltpu.make_async_remote_copy(
            src_ref=src,
            dst_ref=dst,
            send_sem=send,
            recv_sem=recv,
            device_id=target,
            device_id_type=MESH,
        )

    barrier = pltpu.get_barrier_semaphore()
    peers = [sibling, far]
    peers += [at(d, 0, 0, 0) for d in range(1, 4)] + [at(0, d, 0, 0) for d in range(1, 4)]
    peers += [at(0, 0, d, 0) for d in range(1, NZ)]
    mate = 1 - 2 * xl
    peers += [at(mate, 0, d, 0) for d in range(1, NZ)]
    for peer in peers:
        pl.semaphore_signal(barrier, inc=1, device_id=peer, device_id_type=MESH)
    pl.semaphore_wait(barrier, len(peers))

    def clips_copy(target):
        return remote(
            clips_in.at[pl.ds(FD - 4, 4)], clips_halo, halo_send.at[0], halo_recv.at[0], target
        )

    def cot_copy(target):
        return remote(
            cot_in.at[pl.ds(0, 2)], cot_ext.at[pl.ds(HD, 2)], halo_send.at[1], halo_recv.at[1], target
        )

    after = {"tm": (t + 1) % NT, "group": group}
    before = {"tm": (t + NT - 1) % NT, "group": group}

    mine = z % 2

    def cut(full, owner, half, lane, width):
        row = pl.multiple_of(owner * 32 + half * 16, 16)
        return full.at[:, pl.ds(row, 16), pl.ds(lane, width)]

    def owner_of(dy, other):
        h = 1 - xh if other else xh
        return ((y + dy + 4) % 4) * 4 + h * 2 + c

    blocks = [(0, 1), (-1, 0), (1, 0), (2, 0), (-1, 1), (1, 1), (2, 1)]
    ahead, behind = at(0, 0, 1, 0), at(0, 0, -1, 0)
    up2 = at(0, 2, 0, 0)

    def block_copy(w, number, slot, src, dst, to):
        return remote(src, dst, w_send.at[w, number], w_recv.at[w, slot], to)

    def half_copy(w, number, slot, owner, half, to, src=None):
        dst = cut((wd, wt)[w], owner, half, 0, C)
        return block_copy(w, number, slot, dst if src is None else src, dst, to)

    def lane_copy(w, number, slot, owner, half, lane, to):
        dst = cut((wd, wt)[w], owner, half, lane, C // 2)
        return block_copy(w, number, slot, dst, dst, to)

    def whole(w, owner):
        return (wd, wt)[w].at[:, pl.ds(pl.multiple_of(owner * 32, 32), 32), :]

    def first_sends(w):
        own = (wd_own, wt_own)[w]
        half = own.at[:, pl.ds(pl.multiple_of(mine * 16, 16), 16), :]
        return [
            half_copy(w, 0, 0, t, mine, mirror, half),
            half_copy(w, 1, 1, t, mine, up, half),
            half_copy(w, 2, 2, t, mine, down, half),
            half_copy(w, 3, 3, t, mine, up2, half),
            block_copy(w, 4, 21, own, whole(w, t), sibling),
        ]

    def passes(w, index):
        owner = owner_of(*blocks[index])
        sends = []
        if index == 0:
            sends = [
                half_copy(w, 5, 4, owner, mine, up),
                half_copy(w, 6, 5, owner, mine, down),
                half_copy(w, 7, 6, owner, mine, up2),
            ]
        return sends + [
            lane_copy(w, 8 + index, 7 + index, owner, mine, 0, ahead),
            lane_copy(w, 15 + index, 14 + index, owner, mine, C // 2, behind),
            half_copy(w, 22 + index, 22 + index, owner, mine, sibling),
        ]

    def last_pass(w, index):
        owner = owner_of(*blocks[index])
        return half_copy(w, 29 + index, 29 + index, owner, 1 - mine, sibling)

    def own_copy(w):
        return pltpu.make_async_copy((wd_own, wt_own)[w], whole(w, t), l_sem.at[w])

    def arrive(w, *indices):
        for index in indices:
            owner = owner_of(*blocks[index])
            half_copy(w, 0, index, owner, mine, sibling).wait_recv()
            for copy in passes(w, index):
                copy.start()

    def arrive_z(w, *indices):
        for index in indices:
            owner = owner_of(*blocks[index])
            lane_copy(w, 0, 7 + index, owner, 1 - mine, 0, sibling).wait_recv()
            lane_copy(w, 0, 14 + index, owner, 1 - mine, C // 2, sibling).wait_recv()
            last_pass(w, index).start()

    def finish_weights(w):
        own_copy(w).wait()
        other = 1 - 2 * c
        block_copy(w, 0, 21, whole(w, t + other), whole(w, t + other), sibling).wait_recv()
        for index in range(7):
            owner = owner_of(*blocks[index]) + other
            half_copy(w, 0, 22 + index, owner, mine, sibling).wait_recv()
            half_copy(w, 0, 29 + index, owner, 1 - mine, sibling).wait_recv()

    clips_load = pltpu.make_async_copy(clips_in, clips, l_sem.at[2])
    cot_load = pltpu.make_async_copy(cot_in, cot_ext.at[pl.ds(0, HD)], l_sem.at[3])
    clips_load.start()
    cot_load.start()

    @pl.when(t > 0)
    def _():
        cot_copy(before).start()

    for copy in first_sends(0):
        copy.start()

    @pl.when(t < NT - 1)
    def _():
        clips_copy(after).start()

    for copy in first_sends(1):
        copy.start()
    own_copy(0).start()
    own_copy(1).start()

    def length(i):
        return lengths[0, i]

    ends = [length(0)]
    for i in range(1, NC):
        ends.append(ends[-1] + length(i))
    first = t * FD

    def opens(frame):
        f = first + frame
        hit = f == 0
        for end in ends:
            hit = jnp.logical_or(hit, f == end)
        return hit

    opening = {i: opens(i) for i in range(-3, 11)}

    def live(k, frame):
        if k == 0:
            return None
        out = jnp.logical_not(opening[frame])
        if k == 2:
            out = jnp.logical_and(out, jnp.logical_not(opening[frame - 1]))
        return out

    def masked(keep, value):
        return value if keep is None else jnp.where(keep, value, jnp.zeros_like(value))

    def features(block):
        wide = block.astype(F32)
        scale = lax.rsqrt(jnp.mean(wide * wide, axis=-1, keepdims=True) + EPS)
        v = wide * scale
        return (v / (1.0 + jnp.exp(-v))).astype(BF)

    def feature_body(i, _):
        h_ext[4 + i] = features(clips[i])
        return 0

    clips_load.wait()
    lax.fori_loop(0, 4, feature_body, 0)
    arrive(0, 0, 1, 2)
    lax.fori_loop(4, FD, feature_body, 0)
    arrive(0, 3)
    arrive_z(0, 0, 1, 2)
    arrive(0, 4, 5)
    arrive_z(0, 3)
    arrive(0, 6)
    arrive(1, 0)
    arrive_z(0, 4, 5, 6)
    cot_load.wait()

    @pl.when(t < NT - 1)
    def _():
        cot_copy(before).wait_recv()

    @pl.when(t == NT - 1)
    def _():
        cot_ext[pl.ds(HD, 2)] = jnp.zeros((2, S, C), BF)

    finish_weights(0)

    flat0 = cot_ext[pl.ds(0, 5)].reshape(5 * S, C)
    flat1 = cot_ext[pl.ds(1, 5)].reshape(5 * S, C)
    p0 = dot(flat0, wd[0], 1, 1).reshape(5, S, C)
    for j in range(5):
        gh[2 * j] = p0[j]
    p2 = dot(flat1, wd[2], 1, 1).reshape(5, S, C)
    for j in range(5):
        total = gh[2 * j] + masked(live(2, 2 * j + 2), p2[j])
        gh[2 * j] = total
        gm[2 * j] = total.astype(BF)
    p1 = dot(flat1, wd[1], 1, 1).reshape(5, S, C)
    for j in range(5):
        total = masked(live(1, 2 * j + 2), p1[j])
        gh[2 * j + 1] = total
        gm[2 * j + 1] = total.astype(BF)

    arrive(1, 1, 2, 3)
    arrive_z(1, 0, 1, 2)

    @pl.when(t > 0)
    def _():
        clips_copy(after).wait_recv()

    @pl.when(t == 0)
    def _():
        clips_halo[...] = jnp.zeros((4, S, C), BF)

    def halo_body(i, _):
        h_ext[i] = features(clips_halo[i])
        return 0

    lax.fori_loop(0, 4, halo_body, 0)
    for k in range(3):
        for i in range(10):
            taps[k, i] = masked(live(k, i - 2), h_ext[i + 2 - k])

    def core_copy(g, k):
        return remote(
            core_out.at[g, k], core_in.at[g, k], core_send.at[g, k], core_recv.at[g, k], sibling
        )

    def contribute(g, k, value):
        stage[g] = value.reshape(4, 2, 2, 2, 16, C)
        for yy in range(4):
            for h in range(2):
                for l in range(2):
                    acc[g, k, 2 * h + l, yy] = stage[g, yy, h, c, l]
                    core_out[g, k, 2 * h + l, yy] = stage[g, yy, h, 1 - c, l].astype(BF)
        core_copy(g, k).start()

    def merge(g):
        for k in range(3):
            core_copy(g, k).wait_recv()
            acc[g, k] = acc[g, k] + core_in[g, k].astype(F32)

    def lanes(h):
        return pl.ds(h * (C // 2), C // 2)

    def line(h, d):
        return at(d, 0, 0, 0) if h == 0 else at(0, d, 0, 0)

    def outer_copy(g, h, d):
        i = 3 * h + d - 1
        return remote(
            outer_out.at[g, i],
            outer_in.at[g, i],
            outer_send.at[g, i],
            outer_recv.at[g, i],
            line(h, d),
        )

    def inner_copy(g, h, d):
        i = 3 * h + d - 1
        return remote(
            inner_out.at[g, i],
            inner_in.at[g, i],
            inner_send.at[g, i],
            inner_recv.at[g, i],
            line(1 - h, d),
        )

    order = [(h, d) for d in (2, 1, 3) for h in range(2)]

    def outer_start(g):
        for h, d in order:
            if h == 0:
                block = acc[g, :, (x + d) % 4, :, :, lanes(h)]
            else:
                block = acc[g, :, :, (y + d) % 4, :, lanes(h)]
            outer_out[g, 3 * h + d - 1] = block.astype(BF)
            outer_copy(g, h, d).start()

    def inner_start(g):
        for h, d in order:
            outer_copy(g, h, d).wait_recv()
        for h in range(2):
            ref = acc.at[g, :, x] if h == 0 else acc.at[g, :, :, y]
            total = ref[:, :, :, lanes(h)]
            for d in range(1, 4):
                total = total + outer_in[g, 3 * h + d - 1].astype(F32)
            ref[:, :, :, lanes(h)] = total
        for h, d in order:
            if h == 0:
                block = acc[g, :, x, (y + d) % 4, :, lanes(h)]
            else:
                block = acc[g, :, (x + d) % 4, y, :, lanes(h)]
            inner_out[g, 3 * h + d - 1] = block.astype(BF)
            inner_copy(g, h, d).start()

    def z_copy(g, d):
        return remote(
            z_out.at[g, (z + d) % NZ],
            z_in.at[g, d - 1],
            z_send.at[g, d - 1],
            z_recv.at[g, d - 1],
            at(0, 0, d, 0),
        )

    def z_start(g):
        for h, d in order:
            inner_copy(g, h, d).wait_recv()
        for h in range(2):
            total = acc[g, :, x, y, :, lanes(h)]
            for d in range(1, 4):
                total = total + inner_in[g, 3 * h + d - 1].astype(F32)
            for r in range(2):
                for q in range(2):
                    part = total[:, r * 8 : r * 8 + 8, q * 128 : q * 128 + 128]
                    z_wide[g, r * 4 + h * 2 + q] = part
                    z_out[g, r * 4 + h * 2 + q] = part.astype(BF)
        for d in (4, 3, 5, 2, 6, 1, 7):
            z_copy(g, d).start()

    def piece_copy(g, other, d):
        number = other * NZ + d - 1
        return remote(
            piece.at[g],
            pieces.at[g, z, xl],
            p_send.at[g, number],
            p_recv.at[g, number],
            at(mate * other, 0, d, 0),
        )

    sends = [(other, d) for d in (4, 3, 5, 2, 6, 1, 7) for other in (1, 0)] + [(1, 0)]

    def piece_start(g):
        total = z_wide[g, z]
        for d in range(1, NZ):
            z_copy(g, d).wait_recv()
            total = total + z_in[g, d - 1].astype(F32)
        piece[g] = total.astype(BF)
        for other, d in sends:
            piece_copy(g, other, d).start()
        pieces[g, z, xl] = piece[g]

    def time_grad(k):
        left = taps[k, pl.ds(2, FD)].reshape(FD * S, C)
        contribute(0, k, dot(left, gm[pl.ds(0, FD)].reshape(FD * S, C), 0, 0))

    time_grad(0)
    arrive(1, 4, 5)
    arrive_z(1, 3)
    time_grad(1)
    arrive(1, 6)
    time_grad(2)
    arrive_z(1, 4, 5, 6)
    for k in range(1, 3):
        for f in range(FD):
            gtap[k - 1, f] = masked(live(k, f + k), gm[f + k])
    merge(0)
    outer_start(0)
    finish_weights(1)

    def hidden_pair(i, wide):
        total = wide
        for k in range(3):
            total = total + dot(taps[k, pl.ds(i, 2)].reshape(2 * S, C), wt[k], 1, 0)
        hid[pl.ds(i, 2)] = total.astype(BF).reshape(2, S, C)

    hidden_pair(0, clips_halo[pl.ds(2, 2)].astype(F32).reshape(2 * S, C))

    def hidden_body(i, _):
        hidden_pair(2 + 2 * i, clips[pl.ds(2 * i, 2)].astype(F32).reshape(2 * S, C))
        return 0

    lax.fori_loop(0, FD // 2, hidden_body, 0)
    for k in range(3):
        for j in range(HD):
            dtaps[k, j] = masked(live(k, 2 * j), hid[2 * j + 2 - k])

    def down_grad(k):
        contribute(1, k, dot(dtaps[k].reshape(HD * S, C), cot_ext[pl.ds(0, HD)].reshape(HD * S, C), 0, 0))

    down_grad(0)
    down_grad(1)
    down_grad(2)
    total = dot(dtaps[0].reshape(HD * S, C), wd[0], 1, 0)
    total = total + dot(dtaps[1].reshape(HD * S, C), wd[1], 1, 0)
    total = total + dot(dtaps[2].reshape(HD * S, C), wd[2], 1, 0)
    reduced[...] = total.astype(BF).reshape(HD, S, C)
    reduced_store = pltpu.make_async_copy(reduced, reduced_out, l_sem.at[4])
    reduced_store.start()
    merge(1)
    outer_start(1)
    inner_start(0)

    def clips_pair(i, _):
        here = pl.ds(2 * i, 2)
        g = dot(gm[here].reshape(2 * S, C), wt[0], 1, 1)
        g = g + dot(gtap[0, here].reshape(2 * S, C), wt[1], 1, 1)
        g = g + dot(gtap[1, here].reshape(2 * S, C), wt[2], 1, 1)
        wide = clips[here].astype(F32).reshape(2 * S, C)
        scale = lax.rsqrt(jnp.mean(wide * wide, axis=-1, keepdims=True) + EPS)
        v = wide * scale
        sig = 1.0 / (1.0 + jnp.exp(-v))
        d = g * (sig * (1.0 + v * (1.0 - sig)))
        inner = jnp.mean(d * v, axis=-1, keepdims=True)
        grad = (d - v * inner) * scale
        grad_clips[here] = (gh[here].reshape(2 * S, C) + grad).astype(BF).reshape(2, S, C)
        return 0

    lax.fori_loop(0, 2, clips_pair, 0)
    z_start(0)
    lax.fori_loop(2, 3, clips_pair, 0)
    inner_start(1)
    lax.fori_loop(3, 4, clips_pair, 0)
    clips_store = pltpu.make_async_copy(grad_clips, clips_out, l_sem.at[5])
    clips_store.start()
    piece_start(0)
    z_start(1)
    piece_start(1)
    for g in range(2):
        for other, d in sends:
            piece_copy(g, other, d).wait()
    reduced_store.wait()
    clips_store.wait()

    @pl.when(t > 0)
    def _():
        cot_copy(before).wait_send()

    @pl.when(t < NT - 1)
    def _():
        clips_copy(after).wait_send()

    for w in range(2):
        for copy in first_sends(w):
            copy.wait_send()
        for index in range(7):
            for copy in passes(w, index):
                copy.wait_send()
            last_pass(w, index).wait_send()
    for g in range(2):
        for k in range(3):
            core_copy(g, k).wait_send()
        for h, d in order:
            outer_copy(g, h, d).wait_send()
            inner_copy(g, h, d).wait_send()
        for d in range(1, NZ):
            z_copy(g, d).wait_send()


def shards(clips, lengths, w_time, w_down, cotangent):
    vmem = pl.BlockSpec(memory_space=pltpu.VMEM)
    hbm = pl.BlockSpec(memory_space=pl.ANY)
    dma = pltpu.SemaphoreType.DMA
    reduced, grad_clips, pieces = pl.pallas_call(
        kernel,
        out_shape=(
            jax.ShapeDtypeStruct((HD, S, C), BF),
            jax.ShapeDtypeStruct((FD, S, C), BF),
            jax.ShapeDtypeStruct((2, NZ, 2, 3, 8, 128), BF),
        ),
        in_specs=[pl.BlockSpec(memory_space=pltpu.SMEM)] + [hbm] * 4,
        out_specs=(hbm, hbm, vmem),
        scratch_shapes=[
            pltpu.VMEM((FD, S, C), BF),
            pltpu.VMEM((HD, S, C), BF),
            pltpu.VMEM((FD, S, C), BF),
            pltpu.VMEM((3, C, C), BF),
            pltpu.VMEM((3, C, C), BF),
            pltpu.VMEM((4, S, C), BF),
            pltpu.VMEM((HD + 2, S, C), BF),
            pltpu.VMEM((FD + 4, S, C), BF),
            pltpu.VMEM((3, FD + 2, S, C), BF),
            pltpu.VMEM((FD + 2, S, C), F32),
            pltpu.VMEM((FD + 2, S, C), BF),
            pltpu.VMEM((FD + 2, S, C), BF),
            pltpu.VMEM((3, HD, S, C), BF),
            pltpu.VMEM((2, FD, S, C), BF),
            pltpu.VMEM((2, 4, 2, 2, 2, 16, C), F32),
            pltpu.VMEM((2, 3, 4, 4, 16, C), F32),
            pltpu.VMEM((2, 3, 4, 4, 16, C), BF),
            pltpu.VMEM((2, 3, 4, 4, 16, C), BF),
            pltpu.VMEM((2, 6, 3, 4, 16, C // 2), BF),
            pltpu.VMEM((2, 6, 3, 4, 16, C // 2), BF),
            pltpu.VMEM((2, 6, 3, 16, C // 2), BF),
            pltpu.VMEM((2, 6, 3, 16, C // 2), BF),
            pltpu.VMEM((2, NZ, 3, 8, 128), F32),
            pltpu.VMEM((2, NZ, 3, 8, 128), BF),
            pltpu.VMEM((2, NZ - 1, 3, 8, 128), BF),
            pltpu.VMEM((2, 3, 8, 128), BF),
            dma((2, 36)),
            dma((2, 36)),
            dma((2,)),
            dma((2,)),
            dma((2, 3)),
            dma((2, 3)),
            dma((2, 6)),
            dma((2, 6)),
            dma((2, 6)),
            dma((2, 6)),
            dma((2, NZ - 1)),
            dma((2, NZ - 1)),
            dma((2, 2 * NZ)),
            dma((2, 2 * NZ)),
            dma((6,)),
        ],
        name="clip_conv",
        compiler_params=pltpu.CompilerParams(
            collective_id=0, has_side_effects=True, vmem_limit_bytes=60 * 2**20
        ),
    )(lengths, clips[0], w_time, w_down, cotangent[0])
    grads = pieces.reshape(2, 2, 4, 2, 3, 8, 128).transpose(0, 4, 3, 1, 5, 2, 6)
    grads = grads.reshape(2, 3, 32, C).astype(F32)
    return reduced[None], grad_clips[None], grads[0], grads[1]


def solution(mesh):
    in_specs = (
        P("group", "tm", None, None),
        P("group", None),
        P(None, "tm", None),
        P(None, "tm", None),
        P("group", "tm", None, None),
    )
    out_specs = (
        P("group", "tm", None, None),
        P("group", "tm", None, None),
        P(None, "tm", None),
        P(None, "tm", None),
    )
    return jax.shard_map(shards, mesh=mesh, in_specs=in_specs, out_specs=out_specs, check_vma=False)
```

```python
import functools

import jax
import jax.numpy as jnp
from jax import lax
from jax.experimental import pallas as pl
from jax.experimental.pallas import tpu as pltpu
from jax.sharding import PartitionSpec as P

MESH = pl.DeviceIdType.MESH
BF = jnp.bfloat16
F32 = jnp.float32
FD, HD, S, C, NC = 8, 4, 128, 512, 8
NT = 16
NZ = 8
EPS = 1e-06


def dot(a, b, ca, cb):
    return lax.dot_general(a, b, (((ca,), (cb,)), ((), ())), preferred_element_type=F32)


def device(x, y, z, core):
    return {"tm": y * 4 + (x // 2) * 2 + core, "group": z * 2 + x % 2}


def kernel(
    lengths,
    clips_in,
    wt_own,
    wd_own,
    cot_in,
    reduced_out,
    clips_out,
    pieces,
    clips,
    reduced,
    grad_clips,
    wt,
    wd,
    clips_halo,
    cot_ext,
    h_ext,
    taps,
    gh,
    gm,
    hid,
    dtaps,
    gtap,
    stage,
    acc,
    core_out,
    core_in,
    outer_out,
    outer_in,
    inner_out,
    inner_in,
    z_wide,
    z_out,
    z_in,
    piece,
    w_send,
    w_recv,
    halo_send,
    halo_recv,
    core_send,
    core_recv,
    outer_send,
    outer_recv,
    inner_send,
    inner_recv,
    z_send,
    z_recv,
    p_send,
    p_recv,
    l_sem,
):
    t = lax.axis_index("tm")
    group = lax.axis_index("group")
    y, xh, c = t // 4, (t // 2) % 2, t % 2
    z, xl = group // 2, group % 2
    x = 2 * xh + xl

    def at(dx, dy, dz, dc):
        return device((x + dx + 4) % 4, (y + dy + 4) % 4, (z + dz + NZ) % NZ, (c + dc) % 2)

    sibling = at(0, 0, 0, 1)
    up, down = at(0, 1, 0, 0), at(0, -1, 0, 0)
    mirror = device(3 - x, y, z, c)
    step = 2 * c - 1
    far = {"tm": (t + step + NT) % NT, "group": group}

    def remote(src, dst, send, recv, target):
        return pltpu.make_async_remote_copy(
            src_ref=src,
            dst_ref=dst,
            send_sem=send,
            recv_sem=recv,
            device_id=target,
            device_id_type=MESH,
        )

    barrier = pltpu.get_barrier_semaphore()
    peers = [sibling, far]
    peers += [at(d, 0, 0, 0) for d in range(1, 4)] + [at(0, d, 0, 0) for d in range(1, 4)]
    peers += [at(0, 0, d, 0) for d in range(1, NZ)]
    mate = 1 - 2 * xl
    peers += [at(mate, 0, d, 0) for d in range(1, NZ)]
    for peer in peers:
        pl.semaphore_signal(barrier, inc=1, device_id=peer, device_id_type=MESH)
    pl.semaphore_wait(barrier, len(peers))

    def clips_copy(target):
        return remote(
            clips_in.at[pl.ds(FD - 4, 4)], clips_halo, halo_send.at[0], halo_recv.at[0], target
        )

    def cot_copy(target):
        return remote(
            cot_in.at[pl.ds(0, 2)], cot_ext.at[pl.ds(HD, 2)], halo_send.at[1], halo_recv.at[1], target
        )

    after = {"tm": (t + 1) % NT, "group": group}
    before = {"tm": (t + NT - 1) % NT, "group": group}

    mine = z % 2

    def cut(full, owner, half, lane, width):
        row = pl.multiple_of(owner * 32 + half * 16, 16)
        return full.at[:, pl.ds(row, 16), pl.ds(lane, width)]

    def owner_of(dy, other):
        h = 1 - xh if other else xh
        return ((y + dy + 4) % 4) * 4 + h * 2 + c

    blocks = [(0, 1), (-1, 0), (1, 0), (2, 0), (-1, 1), (1, 1), (2, 1)]
    ahead, behind = at(0, 0, 1, 0), at(0, 0, -1, 0)
    up2 = at(0, 2, 0, 0)

    def block_copy(w, number, slot, src, dst, to):
        return remote(src, dst, w_send.at[w, number], w_recv.at[w, slot], to)

    def half_copy(w, number, slot, owner, half, to, src=None):
        dst = cut((wd, wt)[w], owner, half, 0, C)
        return block_copy(w, number, slot, dst if src is None else src, dst, to)

    def lane_copy(w, number, slot, owner, half, lane, to):
        dst = cut((wd, wt)[w], owner, half, lane, C // 2)
        return block_copy(w, number, slot, dst, dst, to)

    def whole(w, owner):
        return (wd, wt)[w].at[:, pl.ds(pl.multiple_of(owner * 32, 32), 32), :]

    def first_sends(w):
        own = (wd_own, wt_own)[w]
        half = own.at[:, pl.ds(pl.multiple_of(mine * 16, 16), 16), :]
        return [
            half_copy(w, 0, 0, t, mine, mirror, half),
            half_copy(w, 1, 1, t, mine, up, half),
            half_copy(w, 2, 2, t, mine, down, half),
            half_copy(w, 3, 3, t, mine, up2, half),
            block_copy(w, 4, 21, own, whole(w, t), sibling),
        ]

    def passes(w, index):
        owner = owner_of(*blocks[index])
        sends = []
        if index == 0:
            sends = [
                half_copy(w, 5, 4, owner, mine, up),
                half_copy(w, 6, 5, owner, mine, down),
                half_copy(w, 7, 6, owner, mine, up2),
            ]
        return sends + [
            lane_copy(w, 8 + index, 7 + index, owner, mine, 0, ahead),
            lane_copy(w, 15 + index, 14 + index, owner, mine, C // 2, behind),
            half_copy(w, 22 + index, 22 + index, owner, mine, sibling),
        ]

    def last_pass(w, index):
        owner = owner_of(*blocks[index])
        return half_copy(w, 29 + index, 29 + index, owner, 1 - mine, sibling)

    def own_copy(w):
        return pltpu.make_async_copy((wd_own, wt_own)[w], whole(w, t), l_sem.at[w])

    def arrive(w, *indices):
        for index in indices:
            owner = owner_of(*blocks[index])
            half_copy(w, 0, index, owner, mine, sibling).wait_recv()
            for copy in passes(w, index):
                copy.start()

    def arrive_z(w, *indices):
        for index in indices:
            owner = owner_of(*blocks[index])
            lane_copy(w, 0, 7 + index, owner, 1 - mine, 0, sibling).wait_recv()
            lane_copy(w, 0, 14 + index, owner, 1 - mine, C // 2, sibling).wait_recv()
            last_pass(w, index).start()

    def finish_weights(w):
        own_copy(w).wait()
        other = 1 - 2 * c
        block_copy(w, 0, 21, whole(w, t + other), whole(w, t + other), sibling).wait_recv()
        for index in range(7):
            owner = owner_of(*blocks[index]) + other
            half_copy(w, 0, 22 + index, owner, mine, sibling).wait_recv()
            half_copy(w, 0, 29 + index, owner, 1 - mine, sibling).wait_recv()

    clips_load = pltpu.make_async_copy(clips_in, clips, l_sem.at[2])
    cot_load = pltpu.make_async_copy(cot_in, cot_ext.at[pl.ds(0, HD)], l_sem.at[3])
    clips_load.start()
    cot_load.start()

    @pl.when(t > 0)
    def _():
        cot_copy(before).start()

    for copy in first_sends(0):
        copy.start()

    @pl.when(t < NT - 1)
    def _():
        clips_copy(after).start()

    own_copy(0).start()
    own_copy(1).start()

    def length(i):
        return lengths[0, i]

    ends = [length(0)]
    for i in range(1, NC):
        ends.append(ends[-1] + length(i))
    first = t * FD

    def opens(frame):
        f = first + frame
        hit = f == 0
        for end in ends:
            hit = jnp.logical_or(hit, f == end)
        return hit

    opening = {i: opens(i) for i in range(-3, 11)}

    def live(k, frame):
        if k == 0:
            return None
        out = jnp.logical_not(opening[frame])
        if k == 2:
            out = jnp.logical_and(out, jnp.logical_not(opening[frame - 1]))
        return out

    def masked(keep, value):
        return value if keep is None else jnp.where(keep, value, jnp.zeros_like(value))

    def features(block):
        wide = block.astype(F32)
        scale = lax.rsqrt(jnp.mean(wide * wide, axis=-1, keepdims=True) + EPS)
        v = wide * scale
        return (v / (1.0 + jnp.exp(-v))).astype(BF)

    def feature_body(i, _):
        h_ext[4 + i] = features(clips[i])
        return 0

    clips_load.wait()
    lax.fori_loop(0, 2, feature_body, 0)
    arrive(0, 0)
    for copy in first_sends(1):
        copy.start()
    lax.fori_loop(2, 4, feature_body, 0)
    arrive(0, 1, 2, 3)
    lax.fori_loop(4, 6, feature_body, 0)
    arrive(1, 0)
    arrive(0, 4, 5, 6)
    lax.fori_loop(6, FD, feature_body, 0)
    arrive(1, 1, 2, 3)
    arrive_z(0, 0, 1, 2, 3, 4, 5, 6)
    cot_load.wait()

    @pl.when(t < NT - 1)
    def _():
        cot_copy(before).wait_recv()

    @pl.when(t == NT - 1)
    def _():
        cot_ext[pl.ds(HD, 2)] = jnp.zeros((2, S, C), BF)

    finish_weights(0)

    flat0 = cot_ext[pl.ds(0, 5)].reshape(5 * S, C)
    flat1 = cot_ext[pl.ds(1, 5)].reshape(5 * S, C)
    p0 = dot(flat0, wd[0], 1, 1).reshape(5, S, C)
    for j in range(5):
        gh[2 * j] = p0[j]
    arrive(1, 4, 5, 6)
    p2 = dot(flat1, wd[2], 1, 1).reshape(5, S, C)
    for j in range(5):
        total = gh[2 * j] + masked(live(2, 2 * j + 2), p2[j])
        gh[2 * j] = total
        gm[2 * j] = total.astype(BF)
    p1 = dot(flat1, wd[1], 1, 1).reshape(5, S, C)
    for j in range(5):
        total = masked(live(1, 2 * j + 2), p1[j])
        gh[2 * j + 1] = total
        gm[2 * j + 1] = total.astype(BF)

    arrive_z(1, 0, 1, 2, 3)

    @pl.when(t > 0)
    def _():
        clips_copy(after).wait_recv()

    @pl.when(t == 0)
    def _():
        clips_halo[...] = jnp.zeros((4, S, C), BF)

    def halo_body(i, _):
        h_ext[i] = features(clips_halo[i])
        return 0

    lax.fori_loop(0, 4, halo_body, 0)
    for k in range(3):
        for i in range(10):
            taps[k, i] = masked(live(k, i - 2), h_ext[i + 2 - k])

    def core_copy(g, k):
        return remote(
            core_out.at[g, k], core_in.at[g, k], core_send.at[g, k], core_recv.at[g, k], sibling
        )

    def contribute(g, k, value):
        stage[g] = value.reshape(4, 2, 2, 2, 16, C)
        for yy in range(4):
            for h in range(2):
                for l in range(2):
                    acc[g, k, 2 * h + l, yy] = stage[g, yy, h, c, l]
                    core_out[g, k, 2 * h + l, yy] = stage[g, yy, h, 1 - c, l].astype(BF)
        core_copy(g, k).start()

    def lanes(h):
        return pl.ds(h * (C // 2), C // 2)

    def line(h, d):
        return at(d, 0, 0, 0) if h == 0 else at(0, d, 0, 0)

    def outer_copy(g, k, h, d):
        i = 3 * h + d - 1
        return remote(
            outer_out.at[g, k, i],
            outer_in.at[g, k, i],
            outer_send.at[g, k, i],
            outer_recv.at[g, k, i],
            line(h, d),
        )

    def inner_copy(g, h, d):
        i = 3 * h + d - 1
        return remote(
            inner_out.at[g, i],
            inner_in.at[g, i],
            inner_send.at[g, i],
            inner_recv.at[g, i],
            line(1 - h, d),
        )

    order = [(h, d) for d in (2, 1, 3) for h in range(2)]

    def reduce_tap(g, k):
        core_copy(g, k).wait_recv()
        acc[g, k] = acc[g, k] + core_in[g, k].astype(F32)
        for h, d in order:
            if h == 0:
                block = acc[g, k, (x + d) % 4, :, :, lanes(h)]
            else:
                block = acc[g, k, :, (y + d) % 4, :, lanes(h)]
            outer_out[g, k, 3 * h + d - 1] = block.astype(BF)
            outer_copy(g, k, h, d).start()

    def inner_start(g):
        for k in range(3):
            for h, d in order:
                outer_copy(g, k, h, d).wait_recv()
            for h in range(2):
                ref = acc.at[g, k, x] if h == 0 else acc.at[g, k, :, y]
                total = ref[:, :, lanes(h)]
                for d in range(1, 4):
                    total = total + outer_in[g, k, 3 * h + d - 1].astype(F32)
                ref[:, :, lanes(h)] = total
        for h, d in order:
            if h == 0:
                block = acc[g, :, x, (y + d) % 4, :, lanes(h)]
            else:
                block = acc[g, :, (x + d) % 4, y, :, lanes(h)]
            inner_out[g, 3 * h + d - 1] = block.astype(BF)
            inner_copy(g, h, d).start()

    def z_copy(g, d):
        return remote(
            z_out.at[g, (z + d) % NZ],
            z_in.at[g, d - 1],
            z_send.at[g, d - 1],
            z_recv.at[g, d - 1],
            at(0, 0, d, 0),
        )

    def z_start(g):
        for h, d in order:
            inner_copy(g, h, d).wait_recv()
        for h in range(2):
            total = acc[g, :, x, y, :, lanes(h)]
            for d in range(1, 4):
                total = total + inner_in[g, 3 * h + d - 1].astype(F32)
            for r in range(2):
                for q in range(2):
                    part = total[:, r * 8 : r * 8 + 8, q * 128 : q * 128 + 128]
                    z_wide[g, r * 4 + h * 2 + q] = part
                    z_out[g, r * 4 + h * 2 + q] = part.astype(BF)
        for d in (4, 3, 5, 2, 6, 1, 7):
            z_copy(g, d).start()

    def piece_copy(g, other, d):
        number = other * NZ + d - 1
        return remote(
            piece.at[g],
            pieces.at[g, z, xl],
            p_send.at[g, number],
            p_recv.at[g, number],
            at(mate * other, 0, d, 0),
        )

    sends = [(other, d) for d in (4, 3, 5, 2, 6, 1, 7) for other in (1, 0)] + [(1, 0)]

    def piece_start(g):
        total = z_wide[g, z]
        for d in range(1, NZ):
            z_copy(g, d).wait_recv()
            total = total + z_in[g, d - 1].astype(F32)
        piece[g] = total.astype(BF)
        for other, d in sends:
            piece_copy(g, other, d).start()
        pieces[g, z, xl] = piece[g]

    def time_grad(k):
        left = taps[k, pl.ds(2, FD)].reshape(FD * S, C)
        contribute(0, k, dot(left, gm[pl.ds(0, FD)].reshape(FD * S, C), 0, 0))

    time_grad(0)
    arrive_z(1, 4, 5, 6)
    time_grad(1)
    reduce_tap(0, 0)
    time_grad(2)
    reduce_tap(0, 1)
    for k in range(1, 3):
        for f in range(FD):
            gtap[k - 1, f] = masked(live(k, f + k), gm[f + k])
    reduce_tap(0, 2)
    finish_weights(1)

    def hidden_pair(i, wide):
        total = wide
        for k in range(3):
            total = total + dot(taps[k, pl.ds(i, 2)].reshape(2 * S, C), wt[k], 1, 0)
        hid[pl.ds(i, 2)] = total.astype(BF).reshape(2, S, C)

    hidden_pair(0, clips_halo[pl.ds(2, 2)].astype(F32).reshape(2 * S, C))

    def hidden_body(i, _):
        hidden_pair(2 + 2 * i, clips[pl.ds(2 * i, 2)].astype(F32).reshape(2 * S, C))
        return 0

    lax.fori_loop(0, FD // 2, hidden_body, 0)
    for k in range(3):
        for j in range(HD):
            dtaps[k, j] = masked(live(k, 2 * j), hid[2 * j + 2 - k])

    def down_grad(k):
        contribute(1, k, dot(dtaps[k].reshape(HD * S, C), cot_ext[pl.ds(0, HD)].reshape(HD * S, C), 0, 0))

    down_grad(0)
    down_grad(1)
    down_grad(2)
    reduce_tap(1, 0)
    total = dot(dtaps[0].reshape(HD * S, C), wd[0], 1, 0)
    total = total + dot(dtaps[1].reshape(HD * S, C), wd[1], 1, 0)
    reduce_tap(1, 1)
    total = total + dot(dtaps[2].reshape(HD * S, C), wd[2], 1, 0)
    reduced[...] = total.astype(BF).reshape(HD, S, C)
    reduced_store = pltpu.make_async_copy(reduced, reduced_out, l_sem.at[4])
    reduced_store.start()
    reduce_tap(1, 2)
    inner_start(0)

    def clips_pair(i, _):
        here = pl.ds(2 * i, 2)
        g = dot(gm[here].reshape(2 * S, C), wt[0], 1, 1)
        g = g + dot(gtap[0, here].reshape(2 * S, C), wt[1], 1, 1)
        g = g + dot(gtap[1, here].reshape(2 * S, C), wt[2], 1, 1)
        wide = clips[here].astype(F32).reshape(2 * S, C)
        scale = lax.rsqrt(jnp.mean(wide * wide, axis=-1, keepdims=True) + EPS)
        v = wide * scale
        sig = 1.0 / (1.0 + jnp.exp(-v))
        d = g * (sig * (1.0 + v * (1.0 - sig)))
        inner = jnp.mean(d * v, axis=-1, keepdims=True)
        grad = (d - v * inner) * scale
        grad_clips[here] = (gh[here].reshape(2 * S, C) + grad).astype(BF).reshape(2, S, C)
        return 0

    lax.fori_loop(0, 2, clips_pair, 0)
    z_start(0)
    lax.fori_loop(2, 3, clips_pair, 0)
    inner_start(1)
    lax.fori_loop(3, 4, clips_pair, 0)
    clips_store = pltpu.make_async_copy(grad_clips, clips_out, l_sem.at[5])
    clips_store.start()
    piece_start(0)
    z_start(1)
    piece_start(1)
    for g in range(2):
        for other, d in sends:
            piece_copy(g, other, d).wait()
    reduced_store.wait()
    clips_store.wait()

    @pl.when(t > 0)
    def _():
        cot_copy(before).wait_send()

    @pl.when(t < NT - 1)
    def _():
        clips_copy(after).wait_send()

    for w in range(2):
        for copy in first_sends(w):
            copy.wait_send()
        for index in range(7):
            for copy in passes(w, index):
                copy.wait_send()
            last_pass(w, index).wait_send()
    for g in range(2):
        for k in range(3):
            core_copy(g, k).wait_send()
        for h, d in order:
            for k in range(3):
                outer_copy(g, k, h, d).wait_send()
            inner_copy(g, h, d).wait_send()
        for d in range(1, NZ):
            z_copy(g, d).wait_send()


def shards(clips, lengths, w_time, w_down, cotangent):
    vmem = pl.BlockSpec(memory_space=pltpu.VMEM)
    hbm = pl.BlockSpec(memory_space=pl.ANY)
    dma = pltpu.SemaphoreType.DMA
    reduced, grad_clips, pieces = pl.pallas_call(
        kernel,
        out_shape=(
            jax.ShapeDtypeStruct((HD, S, C), BF),
            jax.ShapeDtypeStruct((FD, S, C), BF),
            jax.ShapeDtypeStruct((2, NZ, 2, 3, 8, 128), BF),
        ),
        in_specs=[pl.BlockSpec(memory_space=pltpu.SMEM)] + [hbm] * 4,
        out_specs=(hbm, hbm, vmem),
        scratch_shapes=[
            pltpu.VMEM((FD, S, C), BF),
            pltpu.VMEM((HD, S, C), BF),
            pltpu.VMEM((FD, S, C), BF),
            pltpu.VMEM((3, C, C), BF),
            pltpu.VMEM((3, C, C), BF),
            pltpu.VMEM((4, S, C), BF),
            pltpu.VMEM((HD + 2, S, C), BF),
            pltpu.VMEM((FD + 4, S, C), BF),
            pltpu.VMEM((3, FD + 2, S, C), BF),
            pltpu.VMEM((FD + 2, S, C), F32),
            pltpu.VMEM((FD + 2, S, C), BF),
            pltpu.VMEM((FD + 2, S, C), BF),
            pltpu.VMEM((3, HD, S, C), BF),
            pltpu.VMEM((2, FD, S, C), BF),
            pltpu.VMEM((2, 4, 2, 2, 2, 16, C), F32),
            pltpu.VMEM((2, 3, 4, 4, 16, C), F32),
            pltpu.VMEM((2, 3, 4, 4, 16, C), BF),
            pltpu.VMEM((2, 3, 4, 4, 16, C), BF),
            pltpu.VMEM((2, 3, 6, 4, 16, C // 2), BF),
            pltpu.VMEM((2, 3, 6, 4, 16, C // 2), BF),
            pltpu.VMEM((2, 6, 3, 16, C // 2), BF),
            pltpu.VMEM((2, 6, 3, 16, C // 2), BF),
            pltpu.VMEM((2, NZ, 3, 8, 128), F32),
            pltpu.VMEM((2, NZ, 3, 8, 128), BF),
            pltpu.VMEM((2, NZ - 1, 3, 8, 128), BF),
            pltpu.VMEM((2, 3, 8, 128), BF),
            dma((2, 36)),
            dma((2, 36)),
            dma((2,)),
            dma((2,)),
            dma((2, 3)),
            dma((2, 3)),
            dma((2, 3, 6)),
            dma((2, 3, 6)),
            dma((2, 6)),
            dma((2, 6)),
            dma((2, NZ - 1)),
            dma((2, NZ - 1)),
            dma((2, 2 * NZ)),
            dma((2, 2 * NZ)),
            dma((6,)),
        ],
        name="clip_conv",
        compiler_params=pltpu.CompilerParams(
            collective_id=0, has_side_effects=True, vmem_limit_bytes=60 * 2**20
        ),
    )(lengths, clips[0], w_time, w_down, cotangent[0])
    reduced, grad_clips, grad_time, grad_down = pl.pallas_call(
        deliver,
        out_shape=(
            jax.ShapeDtypeStruct((HD, S, C), BF),
            jax.ShapeDtypeStruct((FD, S, C), BF),
            jax.ShapeDtypeStruct((3, 32, C), F32),
            jax.ShapeDtypeStruct((3, 32, C), F32),
        ),
        in_specs=[hbm, hbm, vmem],
        out_specs=(hbm, hbm, vmem, vmem),
        scratch_shapes=[
            pltpu.VMEM((FD + HD, S, C), BF),
            dma((6,)),
            dma((6,)),
        ],
        name="deliver",
        compiler_params=pltpu.CompilerParams(vmem_limit_bytes=60 * 2**20),
    )(reduced, grad_clips, pieces)
    return reduced[None], grad_clips[None], grad_time, grad_down


def deliver(reduced, grad_clips, pieces, reduced_out, clips_out, time_out, down_out, held, load, store):
    def ends(i):
        if i < 4:
            return grad_clips.at[pl.ds(2 * i, 2)], clips_out.at[pl.ds(2 * i, 2)]
        return reduced.at[pl.ds(2 * i - 8, 2)], reduced_out.at[pl.ds(2 * i - 8, 2)]

    loads = [
        pltpu.make_async_copy(ends(i)[0], held.at[pl.ds(2 * i, 2)], load.at[i]) for i in range(6)
    ]
    stores = [
        pltpu.make_async_copy(held.at[pl.ds(2 * i, 2)], ends(i)[1], store.at[i]) for i in range(6)
    ]
    for copy in loads:
        copy.start()
    for g, out in ((0, time_out), (1, down_out)):
        for r in range(2):
            for q in range(4):
                for l in range(2):
                    out[:, l * 16 + r * 8 : l * 16 + r * 8 + 8, q * 128 : q * 128 + 128] = pieces[
                        g, r * 4 + q, l
                    ].astype(F32)
    for i in range(6):
        loads[i].wait()
        stores[i].start()
    for copy in stores:
        copy.wait()


def solution(mesh):
    in_specs = (
        P("group", "tm", None, None),
        P("group", None),
        P(None, "tm", None),
        P(None, "tm", None),
        P("group", "tm", None, None),
    )
    out_specs = (
        P("group", "tm", None, None),
        P("group", "tm", None, None),
        P(None, "tm", None),
        P(None, "tm", None),
    )
    return jax.shard_map(shards, mesh=mesh, in_specs=in_specs, out_specs=out_specs, check_vma=False)
```

```python
import functools

import jax
import jax.numpy as jnp
from jax import lax
from jax.experimental import pallas as pl
from jax.experimental.pallas import tpu as pltpu
from jax.sharding import PartitionSpec as P

MESH = pl.DeviceIdType.MESH
BF = jnp.bfloat16
F32 = jnp.float32
FD, HD, S, C, NC = 8, 4, 128, 512, 8
NT = 16
NZ = 8
EPS = 1e-06


def dot(a, b, ca, cb):
    return lax.dot_general(a, b, (((ca,), (cb,)), ((), ())), preferred_element_type=F32)


def device(x, y, z, core):
    return {"tm": y * 4 + (x // 2) * 2 + core, "group": z * 2 + x % 2}


def kernel(
    lengths_in,
    clips_in,
    wt_own,
    wd_own,
    cot_in,
    reduced,
    grad_clips,
    pieces,
    lengths,
    clips,
    wt,
    wd,
    clips_halo,
    cot_ext,
    h_ext,
    taps,
    gh,
    gm,
    hid,
    dtaps,
    gtap,
    stage,
    acc,
    core_out,
    core_in,
    outer_out,
    outer_in,
    inner_out,
    inner_in,
    z_wide,
    z_out,
    z_in,
    piece,
    w_send,
    w_recv,
    halo_send,
    halo_recv,
    core_send,
    core_recv,
    outer_send,
    outer_recv,
    inner_send,
    inner_recv,
    z_send,
    z_recv,
    p_send,
    p_recv,
    l_sem,
):
    t = lax.axis_index("tm")
    group = lax.axis_index("group")
    y, xh, c = t // 4, (t // 2) % 2, t % 2
    z, xl = group // 2, group % 2
    x = 2 * xh + xl

    def at(dx, dy, dz, dc):
        return device((x + dx + 4) % 4, (y + dy + 4) % 4, (z + dz + NZ) % NZ, (c + dc) % 2)

    sibling = at(0, 0, 0, 1)
    up, down = at(0, 1, 0, 0), at(0, -1, 0, 0)
    mirror = device(3 - x, y, z, c)
    step = 2 * c - 1
    far = {"tm": (t + step + NT) % NT, "group": group}

    def remote(src, dst, send, recv, target):
        return pltpu.make_async_remote_copy(
            src_ref=src,
            dst_ref=dst,
            send_sem=send,
            recv_sem=recv,
            device_id=target,
            device_id_type=MESH,
        )

    lengths_load = pltpu.make_async_copy(lengths_in, lengths, l_sem.at[4])
    lengths_load.start()

    barrier = pltpu.get_barrier_semaphore()
    peers = [sibling, far]
    peers += [at(d, 0, 0, 0) for d in range(1, 4)] + [at(0, d, 0, 0) for d in range(1, 4)]
    peers += [at(0, 0, d, 0) for d in range(1, NZ)]
    mate = 1 - 2 * xl
    peers += [at(mate, 0, d, 0) for d in range(1, NZ)]
    for peer in peers:
        pl.semaphore_signal(barrier, inc=1, device_id=peer, device_id_type=MESH)
    pl.semaphore_wait(barrier, len(peers))

    def clips_copy(f, target):
        return remote(
            clips_in.at[FD - 4 + f], clips_halo.at[f], halo_send.at[f], halo_recv.at[f], target
        )

    def cot_copy(f, target):
        return remote(
            cot_in.at[f], cot_ext.at[HD + f], halo_send.at[4 + f], halo_recv.at[4 + f], target
        )

    after = {"tm": (t + 1) % NT, "group": group}
    before = {"tm": (t + NT - 1) % NT, "group": group}

    mine = z % 2

    def cut(full, owner, half, lane, width):
        row = pl.multiple_of(owner * 32 + half * 16, 16)
        return full.at[:, pl.ds(row, 16), pl.ds(lane, width)]

    def owner_of(dy, other):
        h = 1 - xh if other else xh
        return ((y + dy + 4) % 4) * 4 + h * 2 + c

    blocks = [(0, 1), (-1, 0), (1, 0), (2, 0), (-1, 1), (1, 1), (2, 1)]
    ahead, behind = at(0, 0, 1, 0), at(0, 0, -1, 0)
    up2 = at(0, 2, 0, 0)

    def block_copy(w, number, slot, src, dst, to):
        return remote(src, dst, w_send.at[w, number], w_recv.at[w, slot], to)

    def half_copy(w, number, slot, owner, half, to, src=None):
        dst = cut((wd, wt)[w], owner, half, 0, C)
        return block_copy(w, number, slot, dst if src is None else src, dst, to)

    def lane_copy(w, number, slot, owner, half, lane, to):
        dst = cut((wd, wt)[w], owner, half, lane, C // 2)
        return block_copy(w, number, slot, dst, dst, to)

    def whole(w, owner):
        return (wd, wt)[w].at[:, pl.ds(pl.multiple_of(owner * 32, 32), 32), :]

    def first_sends(w):
        own = (wd_own, wt_own)[w]
        half = own.at[:, pl.ds(pl.multiple_of(mine * 16, 16), 16), :]
        return [
            half_copy(w, 0, 0, t, mine, mirror, half),
            half_copy(w, 1, 1, t, mine, up, half),
            half_copy(w, 2, 2, t, mine, down, half),
            half_copy(w, 3, 3, t, mine, up2, half),
            block_copy(w, 4, 21, own, whole(w, t), sibling),
        ]

    def passes(w, index):
        owner = owner_of(*blocks[index])
        sends = []
        if index == 0:
            sends = [
                half_copy(w, 5, 4, owner, mine, up),
                half_copy(w, 6, 5, owner, mine, down),
                half_copy(w, 7, 6, owner, mine, up2),
            ]
        return sends + [
            lane_copy(w, 8 + index, 7 + index, owner, mine, 0, ahead),
            lane_copy(w, 15 + index, 14 + index, owner, mine, C // 2, behind),
            half_copy(w, 22 + index, 22 + index, owner, mine, sibling),
        ]

    def last_pass(w, index):
        owner = owner_of(*blocks[index])
        return half_copy(w, 29 + index, 29 + index, owner, 1 - mine, sibling)

    def own_copy(w):
        return pltpu.make_async_copy((wd_own, wt_own)[w], whole(w, t), l_sem.at[w])

    def arrive(w, *indices):
        for index in indices:
            owner = owner_of(*blocks[index])
            half_copy(w, 0, index, owner, mine, sibling).wait_recv()
            for copy in passes(w, index):
                copy.start()

    def arrive_z(w, *indices):
        for index in indices:
            owner = owner_of(*blocks[index])
            lane_copy(w, 0, 7 + index, owner, 1 - mine, 0, sibling).wait_recv()
            lane_copy(w, 0, 14 + index, owner, 1 - mine, C // 2, sibling).wait_recv()
            last_pass(w, index).start()

    def finish_weights(w):
        own_copy(w).wait()
        other = 1 - 2 * c
        block_copy(w, 0, 21, whole(w, t + other), whole(w, t + other), sibling).wait_recv()
        for index in range(7):
            owner = owner_of(*blocks[index]) + other
            half_copy(w, 0, 22 + index, owner, mine, sibling).wait_recv()
            half_copy(w, 0, 29 + index, owner, 1 - mine, sibling).wait_recv()

    clips_load = pltpu.make_async_copy(clips_in, clips, l_sem.at[2])
    cot_load = pltpu.make_async_copy(cot_in, cot_ext.at[pl.ds(0, HD)], l_sem.at[3])
    clips_load.start()
    cot_load.start()

    def send_cot(f):
        @pl.when(t > 0)
        def _():
            cot_copy(f, before).start()

    def send_clips(f):
        @pl.when(t < NT - 1)
        def _():
            clips_copy(f, after).start()

    for copy in first_sends(0):
        copy.start()
    send_cot(0)
    own_copy(0).start()
    own_copy(1).start()

    lengths_load.wait()

    def length(i):
        return lengths[0, i]

    ends = [length(0)]
    for i in range(1, NC):
        ends.append(ends[-1] + length(i))
    first = t * FD

    def opens(frame):
        f = first + frame
        hit = f == 0
        for end in ends:
            hit = jnp.logical_or(hit, f == end)
        return hit

    opening = {i: opens(i) for i in range(-3, 11)}

    def live(k, frame):
        if k == 0:
            return None
        out = jnp.logical_not(opening[frame])
        if k == 2:
            out = jnp.logical_and(out, jnp.logical_not(opening[frame - 1]))
        return out

    def masked(keep, value):
        return value if keep is None else jnp.where(keep, value, jnp.zeros_like(value))

    def features(block):
        wide = block.astype(F32)
        scale = lax.rsqrt(jnp.mean(wide * wide, axis=-1, keepdims=True) + EPS)
        v = wide * scale
        return (v / (1.0 + jnp.exp(-v))).astype(BF)

    def feature_body(i, _):
        h_ext[4 + i] = features(clips[i])
        return 0

    clips_load.wait()
    lax.fori_loop(0, 2, feature_body, 0)
    arrive(0, 0)
    send_cot(1)
    for copy in first_sends(1):
        copy.start()
    send_clips(3)
    lax.fori_loop(2, 4, feature_body, 0)
    arrive(0, 1, 2, 3)
    send_clips(2)
    lax.fori_loop(4, 6, feature_body, 0)
    arrive(1, 0)
    send_clips(1)
    arrive(0, 4, 5, 6)
    send_clips(0)
    lax.fori_loop(6, FD, feature_body, 0)
    arrive(1, 1, 2, 3)
    arrive_z(0, 0, 1, 2, 3, 4, 5, 6)
    cot_load.wait()

    @pl.when(t < NT - 1)
    def _():
        cot_copy(0, before).wait_recv()
        cot_copy(1, before).wait_recv()

    @pl.when(t == NT - 1)
    def _():
        cot_ext[pl.ds(HD, 2)] = jnp.zeros((2, S, C), BF)

    finish_weights(0)

    flat0 = cot_ext[pl.ds(0, 5)].reshape(5 * S, C)
    flat1 = cot_ext[pl.ds(1, 5)].reshape(5 * S, C)
    p0 = dot(flat0, wd[0], 1, 1).reshape(5, S, C)
    for j in range(5):
        gh[2 * j] = p0[j]
    arrive(1, 4, 5, 6)
    p2 = dot(flat1, wd[2], 1, 1).reshape(5, S, C)
    for j in range(5):
        total = gh[2 * j] + masked(live(2, 2 * j + 2), p2[j])
        gh[2 * j] = total
        gm[2 * j] = total.astype(BF)
    p1 = dot(flat1, wd[1], 1, 1).reshape(5, S, C)
    for j in range(5):
        total = masked(live(1, 2 * j + 2), p1[j])
        gh[2 * j + 1] = total
        gm[2 * j + 1] = total.astype(BF)

    arrive_z(1, 0, 1, 2, 3)

    @pl.when(t > 0)
    def _():
        for f in range(4):
            clips_copy(f, after).wait_recv()

    @pl.when(t == 0)
    def _():
        clips_halo[...] = jnp.zeros((4, S, C), BF)

    def halo_body(i, _):
        h_ext[i] = features(clips_halo[i])
        return 0

    lax.fori_loop(0, 4, halo_body, 0)
    for k in range(3):
        for i in range(10):
            taps[k, i] = masked(live(k, i - 2), h_ext[i + 2 - k])

    def core_copy(g, k):
        return remote(
            core_out.at[g, k], core_in.at[g, k], core_send.at[g, k], core_recv.at[g, k], sibling
        )

    def contribute(g, k, value):
        stage[g] = value.reshape(4, 2, 2, 2, 16, C)
        for yy in range(4):
            for h in range(2):
                for l in range(2):
                    acc[g, k, 2 * h + l, yy] = stage[g, yy, h, c, l]
                    core_out[g, k, 2 * h + l, yy] = stage[g, yy, h, 1 - c, l].astype(BF)
        core_copy(g, k).start()

    def lanes(h):
        return pl.ds(h * (C // 2), C // 2)

    def line(h, d):
        return at(d, 0, 0, 0) if h == 0 else at(0, d, 0, 0)

    def outer_copy(g, k, h, d):
        i = 3 * h + d - 1
        return remote(
            outer_out.at[g, k, i],
            outer_in.at[g, k, i],
            outer_send.at[g, k, i],
            outer_recv.at[g, k, i],
            line(h, d),
        )

    def inner_copy(g, h, d):
        i = 3 * h + d - 1
        return remote(
            inner_out.at[g, i],
            inner_in.at[g, i],
            inner_send.at[g, i],
            inner_recv.at[g, i],
            line(1 - h, d),
        )

    order = [(h, d) for d in (2, 1, 3) for h in range(2)]

    def reduce_tap(g, k):
        core_copy(g, k).wait_recv()
        acc[g, k] = acc[g, k] + core_in[g, k].astype(F32)
        for h, d in order:
            if h == 0:
                block = acc[g, k, (x + d) % 4, :, :, lanes(h)]
            else:
                block = acc[g, k, :, (y + d) % 4, :, lanes(h)]
            outer_out[g, k, 3 * h + d - 1] = block.astype(BF)
            outer_copy(g, k, h, d).start()

    def inner_start(g):
        for k in range(3):
            for h, d in order:
                outer_copy(g, k, h, d).wait_recv()
            for h in range(2):
                ref = acc.at[g, k, x] if h == 0 else acc.at[g, k, :, y]
                total = ref[:, :, lanes(h)]
                for d in range(1, 4):
                    total = total + outer_in[g, k, 3 * h + d - 1].astype(F32)
                ref[:, :, lanes(h)] = total
        for h, d in order:
            if h == 0:
                block = acc[g, :, x, (y + d) % 4, :, lanes(h)]
            else:
                block = acc[g, :, (x + d) % 4, y, :, lanes(h)]
            inner_out[g, 3 * h + d - 1] = block.astype(BF)
            inner_copy(g, h, d).start()

    def z_copy(g, d):
        return remote(
            z_out.at[g, (z + d) % NZ],
            z_in.at[g, d - 1],
            z_send.at[g, d - 1],
            z_recv.at[g, d - 1],
            at(0, 0, d, 0),
        )

    def z_start(g):
        for h, d in order:
            inner_copy(g, h, d).wait_recv()
        for h in range(2):
            total = acc[g, :, x, y, :, lanes(h)]
            for d in range(1, 4):
                total = total + inner_in[g, 3 * h + d - 1].astype(F32)
            for r in range(2):
                for q in range(2):
                    part = total[:, r * 8 : r * 8 + 8, q * 128 : q * 128 + 128]
                    z_wide[g, r * 4 + h * 2 + q] = part
                    z_out[g, r * 4 + h * 2 + q] = part.astype(BF)
        for d in (4, 3, 5, 2, 6, 1, 7):
            z_copy(g, d).start()

    def piece_copy(g, other, d):
        number = other * NZ + d - 1
        return remote(
            piece.at[g],
            pieces.at[g, z, xl],
            p_send.at[g, number],
            p_recv.at[g, number],
            at(mate * other, 0, d, 0),
        )

    sends = [(other, d) for d in (4, 3, 5, 2, 6, 1, 7) for other in (1, 0)] + [(1, 0)]

    def piece_start(g):
        total = z_wide[g, z]
        for d in range(1, NZ):
            z_copy(g, d).wait_recv()
            total = total + z_in[g, d - 1].astype(F32)
        piece[g] = total.astype(BF)
        for other, d in sends:
            piece_copy(g, other, d).start()
        pieces[g, z, xl] = piece[g]

    def time_grad(k):
        left = taps[k, pl.ds(2, FD)].reshape(FD * S, C)
        contribute(0, k, dot(left, gm[pl.ds(0, FD)].reshape(FD * S, C), 0, 0))

    time_grad(0)
    arrive_z(1, 4, 5, 6)
    time_grad(1)
    reduce_tap(0, 0)
    time_grad(2)
    reduce_tap(0, 1)
    for k in range(1, 3):
        for f in range(FD):
            gtap[k - 1, f] = masked(live(k, f + k), gm[f + k])
    reduce_tap(0, 2)
    finish_weights(1)

    def hidden_pair(i, wide):
        total = wide
        for k in range(3):
            total = total + dot(taps[k, pl.ds(i, 2)].reshape(2 * S, C), wt[k], 1, 0)
        hid[pl.ds(i, 2)] = total.astype(BF).reshape(2, S, C)

    hidden_pair(0, clips_halo[pl.ds(2, 2)].astype(F32).reshape(2 * S, C))

    def hidden_body(i, _):
        hidden_pair(2 + 2 * i, clips[pl.ds(2 * i, 2)].astype(F32).reshape(2 * S, C))
        return 0

    lax.fori_loop(0, FD // 2, hidden_body, 0)
    for k in range(3):
        for j in range(HD):
            dtaps[k, j] = masked(live(k, 2 * j), hid[2 * j + 2 - k])

    def down_grad(k):
        contribute(1, k, dot(dtaps[k].reshape(HD * S, C), cot_ext[pl.ds(0, HD)].reshape(HD * S, C), 0, 0))

    down_grad(0)
    down_grad(1)
    down_grad(2)
    reduce_tap(1, 0)
    total = dot(dtaps[0].reshape(HD * S, C), wd[0], 1, 0)
    total = total + dot(dtaps[1].reshape(HD * S, C), wd[1], 1, 0)
    reduce_tap(1, 1)
    total = total + dot(dtaps[2].reshape(HD * S, C), wd[2], 1, 0)
    reduced[...] = total.astype(BF).reshape(HD, S, C)
    reduce_tap(1, 2)
    inner_start(0)

    def clips_pair(i, _):
        here = pl.ds(2 * i, 2)
        g = dot(gm[here].reshape(2 * S, C), wt[0], 1, 1)
        g = g + dot(gtap[0, here].reshape(2 * S, C), wt[1], 1, 1)
        g = g + dot(gtap[1, here].reshape(2 * S, C), wt[2], 1, 1)
        wide = clips[here].astype(F32).reshape(2 * S, C)
        scale = lax.rsqrt(jnp.mean(wide * wide, axis=-1, keepdims=True) + EPS)
        v = wide * scale
        sig = 1.0 / (1.0 + jnp.exp(-v))
        d = g * (sig * (1.0 + v * (1.0 - sig)))
        inner = jnp.mean(d * v, axis=-1, keepdims=True)
        grad = (d - v * inner) * scale
        grad_clips[here] = (gh[here].reshape(2 * S, C) + grad).astype(BF).reshape(2, S, C)
        return 0

    lax.fori_loop(0, 2, clips_pair, 0)
    z_start(0)
    lax.fori_loop(2, 3, clips_pair, 0)
    inner_start(1)
    lax.fori_loop(3, 4, clips_pair, 0)
    piece_start(0)
    z_start(1)
    piece_start(1)
    for g in range(2):
        for other, d in sends:
            piece_copy(g, other, d).wait()

    @pl.when(t > 0)
    def _():
        cot_copy(0, before).wait_send()
        cot_copy(1, before).wait_send()

    @pl.when(t < NT - 1)
    def _():
        for f in range(4):
            clips_copy(f, after).wait_send()

    for w in range(2):
        for copy in first_sends(w):
            copy.wait_send()
        for index in range(7):
            for copy in passes(w, index):
                copy.wait_send()
            last_pass(w, index).wait_send()
    for g in range(2):
        for k in range(3):
            core_copy(g, k).wait_send()
        for h, d in order:
            for k in range(3):
                outer_copy(g, k, h, d).wait_send()
            inner_copy(g, h, d).wait_send()
        for d in range(1, NZ):
            z_copy(g, d).wait_send()


def shards(clips, lengths, w_time, w_down, cotangent):
    vmem = pl.BlockSpec(memory_space=pltpu.VMEM)
    hbm = pl.BlockSpec(memory_space=pltpu.HBM)
    pin = pltpu.with_memory_space_constraint
    dma = pltpu.SemaphoreType.DMA
    reduced, grad_clips, pieces = pl.pallas_call(
        kernel,
        out_shape=(
            jax.ShapeDtypeStruct((HD, S, C), BF),
            jax.ShapeDtypeStruct((FD, S, C), BF),
            jax.ShapeDtypeStruct((2, NZ, 2, 3, 8, 128), BF),
        ),
        in_specs=[hbm] * 5,
        out_specs=(vmem, vmem, vmem),
        scratch_shapes=[
            pltpu.SMEM((1, NC), jnp.int32),
            pltpu.VMEM((FD, S, C), BF),
            pltpu.VMEM((3, C, C), BF),
            pltpu.VMEM((3, C, C), BF),
            pltpu.VMEM((4, S, C), BF),
            pltpu.VMEM((HD + 2, S, C), BF),
            pltpu.VMEM((FD + 4, S, C), BF),
            pltpu.VMEM((3, FD + 2, S, C), BF),
            pltpu.VMEM((FD + 2, S, C), F32),
            pltpu.VMEM((FD + 2, S, C), BF),
            pltpu.VMEM((FD + 2, S, C), BF),
            pltpu.VMEM((3, HD, S, C), BF),
            pltpu.VMEM((2, FD, S, C), BF),
            pltpu.VMEM((2, 4, 2, 2, 2, 16, C), F32),
            pltpu.VMEM((2, 3, 4, 4, 16, C), F32),
            pltpu.VMEM((2, 3, 4, 4, 16, C), BF),
            pltpu.VMEM((2, 3, 4, 4, 16, C), BF),
            pltpu.VMEM((2, 3, 6, 4, 16, C // 2), BF),
            pltpu.VMEM((2, 3, 6, 4, 16, C // 2), BF),
            pltpu.VMEM((2, 6, 3, 16, C // 2), BF),
            pltpu.VMEM((2, 6, 3, 16, C // 2), BF),
            pltpu.VMEM((2, NZ, 3, 8, 128), F32),
            pltpu.VMEM((2, NZ, 3, 8, 128), BF),
            pltpu.VMEM((2, NZ - 1, 3, 8, 128), BF),
            pltpu.VMEM((2, 3, 8, 128), BF),
            dma((2, 36)),
            dma((2, 36)),
            dma((6,)),
            dma((6,)),
            dma((2, 3)),
            dma((2, 3)),
            dma((2, 3, 6)),
            dma((2, 3, 6)),
            dma((2, 6)),
            dma((2, 6)),
            dma((2, NZ - 1)),
            dma((2, NZ - 1)),
            dma((2, 2 * NZ)),
            dma((2, 2 * NZ)),
            dma((5,)),
        ],
        name="clip_conv",
        compiler_params=pltpu.CompilerParams(
            collective_id=0, has_side_effects=True, vmem_limit_bytes=44 * 2**20
        ),
    )(*(pin(a, pltpu.HBM) for a in (lengths, clips[0], w_time, w_down, cotangent[0])))
    reduced, grad_clips, grad_time, grad_down = pl.pallas_call(
        deliver,
        out_shape=(
            jax.ShapeDtypeStruct((HD, S, C), BF),
            jax.ShapeDtypeStruct((FD, S, C), BF),
            jax.ShapeDtypeStruct((3, 32, C), F32),
            jax.ShapeDtypeStruct((3, 32, C), F32),
        ),
        in_specs=[vmem] * 3,
        out_specs=(hbm,) * 4,
        scratch_shapes=[
            pltpu.VMEM((3, 32, C), F32),
            pltpu.VMEM((3, 32, C), F32),
            dma((4,)),
        ],
        name="deliver",
        compiler_params=pltpu.CompilerParams(vmem_limit_bytes=16 * 2**20),
    )(reduced, grad_clips, pieces)
    return reduced[None], grad_clips[None], grad_time, grad_down


def deliver(reduced, grad_clips, pieces, reduced_out, clips_out, time_out, down_out, time, down, sem):
    pairs = ((grad_clips, clips_out), (reduced, reduced_out), (time, time_out), (down, down_out))
    stores = [pltpu.make_async_copy(a, b, sem.at[i]) for i, (a, b) in enumerate(pairs)]
    stores[0].start()
    stores[1].start()
    for g, full in ((0, time), (1, down)):
        for r in range(2):
            for q in range(4):
                for l in range(2):
                    full[:, l * 16 + r * 8 : l * 16 + r * 8 + 8, q * 128 : q * 128 + 128] = pieces[
                        g, r * 4 + q, l
                    ].astype(F32)
        stores[2 + g].start()
    for copy in stores:
        copy.wait()


def solution(mesh):
    in_specs = (
        P("group", "tm", None, None),
        P("group", None),
        P(None, "tm", None),
        P(None, "tm", None),
        P("group", "tm", None, None),
    )
    out_specs = (
        P("group", "tm", None, None),
        P("group", "tm", None, None),
        P(None, "tm", None),
        P(None, "tm", None),
    )
    return jax.shard_map(shards, mesh=mesh, in_specs=in_specs, out_specs=out_specs, check_vma=False)
```

```python
import functools

import jax
import jax.numpy as jnp
from jax import lax
from jax.experimental import pallas as pl
from jax.experimental.pallas import tpu as pltpu
from jax.sharding import PartitionSpec as P

MESH = pl.DeviceIdType.MESH
BF = jnp.bfloat16
F32 = jnp.float32
FD, HD, S, C, NC = 8, 4, 128, 512, 8
NT = 16
NZ = 8
EPS = 1e-06


def dot(a, b, ca, cb):
    return lax.dot_general(a, b, (((ca,), (cb,)), ((), ())), preferred_element_type=F32)


def device(x, y, z, core):
    return {"tm": y * 4 + (x // 2) * 2 + core, "group": z * 2 + x % 2}


def kernel(
    lengths_in,
    clips_in,
    wt_own,
    wd_own,
    cot_in,
    reduced,
    grad_clips,
    pieces,
    lengths,
    clips,
    wt,
    wd,
    clips_halo,
    cot_ext,
    h_ext,
    taps,
    gh,
    gm,
    hid,
    dtaps,
    gtap,
    stage,
    acc,
    core_out,
    core_in,
    outer_out,
    outer_in,
    inner_out,
    inner_in,
    z_wide,
    z_out,
    z_in,
    piece,
    w_send,
    w_recv,
    halo_send,
    halo_recv,
    core_send,
    core_recv,
    outer_send,
    outer_recv,
    inner_send,
    inner_recv,
    z_send,
    z_recv,
    p_send,
    p_recv,
    l_sem,
):
    t = lax.axis_index("tm")
    group = lax.axis_index("group")
    y, xh, c = t // 4, (t // 2) % 2, t % 2
    z, xl = group // 2, group % 2
    x = 2 * xh + xl

    def at(dx, dy, dz, dc):
        return device((x + dx + 4) % 4, (y + dy + 4) % 4, (z + dz + NZ) % NZ, (c + dc) % 2)

    sibling = at(0, 0, 0, 1)
    up, down = at(0, 1, 0, 0), at(0, -1, 0, 0)
    mirror = device(3 - x, y, z, c)
    step = 2 * c - 1
    far = {"tm": (t + step + NT) % NT, "group": group}

    def remote(src, dst, send, recv, target):
        return pltpu.make_async_remote_copy(
            src_ref=src,
            dst_ref=dst,
            send_sem=send,
            recv_sem=recv,
            device_id=target,
            device_id_type=MESH,
        )

    lengths_load = pltpu.make_async_copy(lengths_in, lengths, l_sem.at[4])
    lengths_load.start()

    barrier = pltpu.get_barrier_semaphore()
    peers = [sibling, far]
    peers += [at(d, 0, 0, 0) for d in range(1, 4)] + [at(0, d, 0, 0) for d in range(1, 4)]
    peers += [at(0, 0, d, 0) for d in range(1, NZ)]
    mate = 1 - 2 * xl
    peers += [at(mate, 0, d, 0) for d in range(1, NZ)]
    for peer in peers:
        pl.semaphore_signal(barrier, inc=1, device_id=peer, device_id_type=MESH)
    pl.semaphore_wait(barrier, len(peers))

    def clips_copy(f, target):
        return remote(
            clips_in.at[FD - 4 + f], clips_halo.at[f], halo_send.at[f], halo_recv.at[f], target
        )

    def cot_copy(f, target):
        return remote(
            cot_in.at[f], cot_ext.at[HD + f], halo_send.at[4 + f], halo_recv.at[4 + f], target
        )

    after = {"tm": (t + 1) % NT, "group": group}
    before = {"tm": (t + NT - 1) % NT, "group": group}

    mine = (z + xl) % 2

    def cut(full, owner, half, lane, width):
        row = pl.multiple_of(owner * 32 + half * 16, 16)
        return full.at[:, pl.ds(row, 16), pl.ds(lane, width)]

    def owner_of(dy, other):
        h = 1 - xh if other else xh
        return ((y + dy + 4) % 4) * 4 + h * 2 + c

    blocks = [(0, 1), (-1, 0), (1, 0), (2, 0), (-1, 1), (1, 1), (2, 1)]
    ahead, behind, beside = at(0, 0, 1, 0), at(0, 0, -1, 0), at(mate, 0, 0, 0)
    up2 = at(0, 2, 0, 0)

    def block_copy(w, number, slot, src, dst, to):
        return remote(src, dst, w_send.at[w, number], w_recv.at[w, slot], to)

    def half_copy(w, number, slot, owner, half, to, src=None):
        dst = cut((wd, wt)[w], owner, half, 0, C)
        return block_copy(w, number, slot, dst if src is None else src, dst, to)

    def tap_copy(w, number, slot, owner, half, tap, to):
        row = pl.multiple_of(owner * 32 + half * 16, 16)
        dst = (wd, wt)[w].at[tap, pl.ds(row, 16), :]
        return block_copy(w, number, slot, dst, dst, to)

    def whole(w, owner):
        return (wd, wt)[w].at[:, pl.ds(pl.multiple_of(owner * 32, 32), 32), :]

    def first_sends(w):
        own = (wd_own, wt_own)[w]
        half = own.at[:, pl.ds(pl.multiple_of(mine * 16, 16), 16), :]
        rest = own.at[:, pl.ds(pl.multiple_of(16 - mine * 16, 16), 16), :]
        return [
            half_copy(w, 0, 0, t, 1 - mine, mirror, rest),
            half_copy(w, 1, 1, t, mine, up, half),
            half_copy(w, 2, 2, t, mine, down, half),
            half_copy(w, 3, 3, t, mine, up2, half),
            block_copy(w, 4, 21, own, whole(w, t), sibling),
        ]

    def passes(w, index):
        owner = owner_of(*blocks[index])
        sends = []
        if index == 0:
            sends = [
                half_copy(w, 5, 4, owner, mine, up),
                half_copy(w, 6, 5, owner, mine, down),
                half_copy(w, 7, 6, owner, mine, up2),
            ]
        return sends + [
            tap_copy(w, 8 + index, 7 + index, owner, mine, 0, ahead),
            tap_copy(w, 15 + index, 14 + index, owner, mine, 2, behind),
            tap_copy(w, 36 + index, 36 + index, owner, mine, 1, beside),
            half_copy(w, 22 + index, 22 + index, owner, mine, sibling),
        ]

    def last_pass(w, index):
        owner = owner_of(*blocks[index])
        return half_copy(w, 29 + index, 29 + index, owner, 1 - mine, sibling)

    def own_copy(w):
        return pltpu.make_async_copy((wd_own, wt_own)[w], whole(w, t), l_sem.at[w])

    def arrive(w, *indices):
        for index in indices:
            owner = owner_of(*blocks[index])
            half_copy(w, 0, index, owner, mine, sibling).wait_recv()
            for copy in passes(w, index):
                copy.start()

    def arrive_z(w, *indices):
        for index in indices:
            owner = owner_of(*blocks[index])
            tap_copy(w, 0, 7 + index, owner, 1 - mine, 0, sibling).wait_recv()
            tap_copy(w, 0, 14 + index, owner, 1 - mine, 2, sibling).wait_recv()
            tap_copy(w, 0, 36 + index, owner, 1 - mine, 1, sibling).wait_recv()
            last_pass(w, index).start()

    def finish_weights(w):
        own_copy(w).wait()
        other = 1 - 2 * c
        block_copy(w, 0, 21, whole(w, t + other), whole(w, t + other), sibling).wait_recv()
        for index in range(7):
            owner = owner_of(*blocks[index]) + other
            half_copy(w, 0, 22 + index, owner, mine, sibling).wait_recv()
            half_copy(w, 0, 29 + index, owner, 1 - mine, sibling).wait_recv()

    clips_load = pltpu.make_async_copy(clips_in, clips, l_sem.at[2])
    cot_load = pltpu.make_async_copy(cot_in, cot_ext.at[pl.ds(0, HD)], l_sem.at[3])
    clips_load.start()
    cot_load.start()

    def send_cot(f):
        @pl.when(t > 0)
        def _():
            cot_copy(f, before).start()

    def send_clips(f):
        @pl.when(t < NT - 1)
        def _():
            clips_copy(f, after).start()

    for copy in first_sends(0):
        copy.start()
    send_cot(0)
    own_copy(0).start()
    own_copy(1).start()

    lengths_load.wait()

    def length(i):
        return lengths[0, i]

    ends = [length(0)]
    for i in range(1, NC):
        ends.append(ends[-1] + length(i))
    first = t * FD

    def opens(frame):
        f = first + frame
        hit = f == 0
        for end in ends:
            hit = jnp.logical_or(hit, f == end)
        return hit

    opening = {i: opens(i) for i in range(-3, 11)}

    def live(k, frame):
        if k == 0:
            return None
        out = jnp.logical_not(opening[frame])
        if k == 2:
            out = jnp.logical_and(out, jnp.logical_not(opening[frame - 1]))
        return out

    def masked(keep, value):
        return value if keep is None else jnp.where(keep, value, jnp.zeros_like(value))

    def features(block):
        wide = block.astype(F32)
        scale = lax.rsqrt(jnp.mean(wide * wide, axis=-1, keepdims=True) + EPS)
        v = wide * scale
        return (v / (1.0 + jnp.exp(-v))).astype(BF)

    def feature_body(i, _):
        h_ext[4 + i] = features(clips[i])
        return 0

    clips_load.wait()
    lax.fori_loop(0, 2, feature_body, 0)
    arrive(0, 0)
    send_cot(1)
    for copy in first_sends(1):
        copy.start()
    lax.fori_loop(2, 4, feature_body, 0)
    arrive(0, 1, 2, 3)
    send_clips(3)
    lax.fori_loop(4, 6, feature_body, 0)
    arrive(1, 0)
    arrive(0, 4, 5, 6)
    send_clips(2)
    lax.fori_loop(6, FD, feature_body, 0)
    arrive(1, 1, 2, 3)
    send_clips(1)
    send_clips(0)
    arrive_z(0, 0, 1, 2, 3, 4, 5, 6)
    cot_load.wait()

    @pl.when(t < NT - 1)
    def _():
        cot_copy(0, before).wait_recv()
        cot_copy(1, before).wait_recv()

    @pl.when(t == NT - 1)
    def _():
        cot_ext[pl.ds(HD, 2)] = jnp.zeros((2, S, C), BF)

    finish_weights(0)

    flat0 = cot_ext[pl.ds(0, 5)].reshape(5 * S, C)
    flat1 = cot_ext[pl.ds(1, 5)].reshape(5 * S, C)
    p0 = dot(flat0, wd[0], 1, 1).reshape(5, S, C)
    for j in range(5):
        gh[2 * j] = p0[j]
    arrive(1, 4, 5, 6)
    p2 = dot(flat1, wd[2], 1, 1).reshape(5, S, C)
    for j in range(5):
        total = gh[2 * j] + masked(live(2, 2 * j + 2), p2[j])
        gh[2 * j] = total
        gm[2 * j] = total.astype(BF)
    p1 = dot(flat1, wd[1], 1, 1).reshape(5, S, C)
    for j in range(5):
        total = masked(live(1, 2 * j + 2), p1[j])
        gh[2 * j + 1] = total
        gm[2 * j + 1] = total.astype(BF)

    arrive_z(1, 0, 1, 2, 3)

    def core_copy(g, k):
        return remote(
            core_out.at[g, k], core_in.at[g, k], core_send.at[g, k], core_recv.at[g, k], sibling
        )

    def contribute(g, k, value):
        stage[g] = value.reshape(4, 2, 2, 2, 16, C)
        for yy in range(4):
            for h in range(2):
                for l in range(2):
                    acc[g, k, 2 * h + l, yy] = stage[g, yy, h, c, l]
                    core_out[g, k, 2 * h + l, yy] = stage[g, yy, h, 1 - c, l].astype(BF)
        core_copy(g, k).start()

    def lanes(h):
        return pl.ds(h * (C // 2), C // 2)

    def line(h, d):
        return at(d, 0, 0, 0) if h == 0 else at(0, d, 0, 0)

    def outer_copy(g, k, h, d):
        i = 3 * h + d - 1
        return remote(
            outer_out.at[g, k, i],
            outer_in.at[g, k, i],
            outer_send.at[g, k, i],
            outer_recv.at[g, k, i],
            line(h, d),
        )

    def inner_copy(g, k, h, d):
        i = 3 * h + d - 1
        return remote(
            inner_out.at[g, k, i],
            inner_in.at[g, k, i],
            inner_send.at[g, k, i],
            inner_recv.at[g, k, i],
            line(1 - h, d),
        )

    order = [(h, d) for d in (2, 1, 3) for h in range(2)]

    def reduce_tap(g, k):
        core_copy(g, k).wait_recv()
        acc[g, k] = acc[g, k] + core_in[g, k].astype(F32)
        for h, d in order:
            if h == 0:
                block = acc[g, k, (x + d) % 4, :, :, lanes(h)]
            else:
                block = acc[g, k, :, (y + d) % 4, :, lanes(h)]
            outer_out[g, k, 3 * h + d - 1] = block.astype(BF)
            outer_copy(g, k, h, d).start()

    def inner_start(g, k):
        for h, d in order:
            outer_copy(g, k, h, d).wait_recv()
        for h in range(2):
            ref = acc.at[g, k, x] if h == 0 else acc.at[g, k, :, y]
            total = ref[:, :, lanes(h)]
            for d in range(1, 4):
                total = total + outer_in[g, k, 3 * h + d - 1].astype(F32)
            ref[:, :, lanes(h)] = total
        for h, d in order:
            if h == 0:
                block = acc[g, k, x, (y + d) % 4, :, lanes(h)]
            else:
                block = acc[g, k, (x + d) % 4, y, :, lanes(h)]
            inner_out[g, k, 3 * h + d - 1] = block.astype(BF)
            inner_copy(g, k, h, d).start()

    def z_copy(g, d):
        return remote(
            z_out.at[g, (z + d) % NZ],
            z_in.at[g, d - 1],
            z_send.at[g, d - 1],
            z_recv.at[g, d - 1],
            at(0, 0, d, 0),
        )

    def z_start(g):
        for k in range(3):
            for h, d in order:
                inner_copy(g, k, h, d).wait_recv()
            for h in range(2):
                total = acc[g, k, x, y, :, lanes(h)]
                for d in range(1, 4):
                    total = total + inner_in[g, k, 3 * h + d - 1].astype(F32)
                for r in range(2):
                    for q in range(2):
                        part = total[r * 8 : r * 8 + 8, q * 128 : q * 128 + 128]
                        z_wide[g, r * 4 + h * 2 + q, k] = part
                        z_out[g, r * 4 + h * 2 + q, k] = part.astype(BF)
        for d in (4, 3, 5, 2, 6, 1, 7):
            z_copy(g, d).start()

    def piece_copy(g, other, d):
        number = other * NZ + d - 1
        return remote(
            piece.at[g],
            pieces.at[g, z, xl],
            p_send.at[g, number],
            p_recv.at[g, number],
            at(mate * other, 0, d, 0),
        )

    sends = [(other, d) for d in (4, 3, 5, 2, 6, 1, 7) for other in (1, 0)] + [(1, 0)]

    def piece_start(g):
        total = z_wide[g, z]
        for d in range(1, NZ):
            z_copy(g, d).wait_recv()
            total = total + z_in[g, d - 1].astype(F32)
        piece[g] = total.astype(BF)
        for other, d in sends:
            piece_copy(g, other, d).start()
        pieces[g, z, xl] = piece[g]

    def time_grad(k):
        left = h_ext[pl.ds(4, FD)] if k == 0 else taps[k, pl.ds(2, FD)]
        left = left.reshape(FD * S, C)
        contribute(0, k, dot(left, gm[pl.ds(0, FD)].reshape(FD * S, C), 0, 0))

    time_grad(0)
    arrive_z(1, 4, 5, 6)

    @pl.when(t > 0)
    def _():
        for f in range(4):
            clips_copy(f, after).wait_recv()

    @pl.when(t == 0)
    def _():
        clips_halo[...] = jnp.zeros((4, S, C), BF)

    def halo_body(i, _):
        h_ext[i] = features(clips_halo[i])
        return 0

    lax.fori_loop(0, 4, halo_body, 0)
    for k in range(3):
        for i in range(10):
            taps[k, i] = masked(live(k, i - 2), h_ext[i + 2 - k])

    time_grad(1)
    reduce_tap(0, 0)
    time_grad(2)
    reduce_tap(0, 1)
    for k in range(1, 3):
        for f in range(FD):
            gtap[k - 1, f] = masked(live(k, f + k), gm[f + k])
    reduce_tap(0, 2)
    finish_weights(1)

    def hidden_three(i, wide):
        total = wide.astype(F32).reshape(3 * S, C)
        for k in range(3):
            total = total + dot(taps[k, pl.ds(i, 3)].reshape(3 * S, C), wt[k], 1, 0)
        hid[pl.ds(i, 3)] = total.astype(BF).reshape(3, S, C)

    hidden_three(0, jnp.concatenate([clips_halo[pl.ds(2, 2)], clips[pl.ds(0, 1)]], axis=0))
    hidden_three(3, clips[pl.ds(1, 3)])
    hidden_three(6, clips[pl.ds(4, 3)])
    for k in range(3):
        for j in range(HD):
            dtaps[k, j] = masked(live(k, 2 * j), hid[2 * j + 2 - k])

    def down_grad(k):
        contribute(1, k, dot(dtaps[k].reshape(HD * S, C), cot_ext[pl.ds(0, HD)].reshape(HD * S, C), 0, 0))

    down_grad(0)
    down_grad(1)
    down_grad(2)
    reduce_tap(1, 0)
    reduce_tap(1, 1)
    inner_start(0, 0)
    reduce_tap(1, 2)
    inner_start(0, 1)
    inner_start(0, 2)
    total = dot(dtaps[0].reshape(HD * S, C), wd[0], 1, 0)
    total = total + dot(dtaps[1].reshape(HD * S, C), wd[1], 1, 0)
    total = total + dot(dtaps[2].reshape(HD * S, C), wd[2], 1, 0)
    reduced[...] = total.astype(BF).reshape(HD, S, C)

    def clips_pair(i, _):
        here = pl.ds(2 * i, 2)
        g = dot(gm[here].reshape(2 * S, C), wt[0], 1, 1)
        g = g + dot(gtap[0, here].reshape(2 * S, C), wt[1], 1, 1)
        g = g + dot(gtap[1, here].reshape(2 * S, C), wt[2], 1, 1)
        wide = clips[here].astype(F32).reshape(2 * S, C)
        scale = lax.rsqrt(jnp.mean(wide * wide, axis=-1, keepdims=True) + EPS)
        v = wide * scale
        sig = 1.0 / (1.0 + jnp.exp(-v))
        d = g * (sig * (1.0 + v * (1.0 - sig)))
        inner = jnp.mean(d * v, axis=-1, keepdims=True)
        grad = (d - v * inner) * scale
        grad_clips[here] = (gh[here].reshape(2 * S, C) + grad).astype(BF).reshape(2, S, C)
        return 0

    z_start(0)
    inner_start(1, 0)
    lax.fori_loop(0, 1, clips_pair, 0)
    inner_start(1, 1)
    inner_start(1, 2)
    lax.fori_loop(1, 2, clips_pair, 0)
    z_start(1)
    piece_start(0)
    lax.fori_loop(2, 3, clips_pair, 0)
    piece_start(1)
    lax.fori_loop(3, 4, clips_pair, 0)
    for g in range(2):
        for other, d in sends:
            piece_copy(g, other, d).wait()

    @pl.when(t > 0)
    def _():
        cot_copy(0, before).wait_send()
        cot_copy(1, before).wait_send()

    @pl.when(t < NT - 1)
    def _():
        for f in range(4):
            clips_copy(f, after).wait_send()

    for w in range(2):
        for copy in first_sends(w):
            copy.wait_send()
        for index in range(7):
            for copy in passes(w, index):
                copy.wait_send()
            last_pass(w, index).wait_send()
    for g in range(2):
        for k in range(3):
            core_copy(g, k).wait_send()
        for h, d in order:
            for k in range(3):
                outer_copy(g, k, h, d).wait_send()
                inner_copy(g, k, h, d).wait_send()
        for d in range(1, NZ):
            z_copy(g, d).wait_send()


def shards(clips, lengths, w_time, w_down, cotangent):
    vmem = pl.BlockSpec(memory_space=pltpu.VMEM)
    hbm = pl.BlockSpec(memory_space=pltpu.HBM)
    pin = pltpu.with_memory_space_constraint
    dma = pltpu.SemaphoreType.DMA
    reduced, grad_clips, pieces = pl.pallas_call(
        kernel,
        out_shape=(
            jax.ShapeDtypeStruct((HD, S, C), BF),
            jax.ShapeDtypeStruct((FD, S, C), BF),
            jax.ShapeDtypeStruct((2, NZ, 2, 3, 8, 128), BF),
        ),
        in_specs=[hbm] * 5,
        out_specs=(vmem, vmem, vmem),
        scratch_shapes=[
            pltpu.SMEM((1, NC), jnp.int32),
            pltpu.VMEM((FD, S, C), BF),
            pltpu.VMEM((3, C, C), BF),
            pltpu.VMEM((3, C, C), BF),
            pltpu.VMEM((4, S, C), BF),
            pltpu.VMEM((HD + 2, S, C), BF),
            pltpu.VMEM((FD + 4, S, C), BF),
            pltpu.VMEM((3, FD + 2, S, C), BF),
            pltpu.VMEM((FD + 2, S, C), F32),
            pltpu.VMEM((FD + 2, S, C), BF),
            pltpu.VMEM((FD + 1, S, C), BF),
            pltpu.VMEM((3, HD, S, C), BF),
            pltpu.VMEM((2, FD, S, C), BF),
            pltpu.VMEM((2, 4, 2, 2, 2, 16, C), F32),
            pltpu.VMEM((2, 3, 4, 4, 16, C), F32),
            pltpu.VMEM((2, 3, 4, 4, 16, C), BF),
            pltpu.VMEM((2, 3, 4, 4, 16, C), BF),
            pltpu.VMEM((2, 3, 6, 4, 16, C // 2), BF),
            pltpu.VMEM((2, 3, 6, 4, 16, C // 2), BF),
            pltpu.VMEM((2, 3, 6, 16, C // 2), BF),
            pltpu.VMEM((2, 3, 6, 16, C // 2), BF),
            pltpu.VMEM((2, NZ, 3, 8, 128), F32),
            pltpu.VMEM((2, NZ, 3, 8, 128), BF),
            pltpu.VMEM((2, NZ - 1, 3, 8, 128), BF),
            pltpu.VMEM((2, 3, 8, 128), BF),
            dma((2, 43)),
            dma((2, 43)),
            dma((6,)),
            dma((6,)),
            dma((2, 3)),
            dma((2, 3)),
            dma((2, 3, 6)),
            dma((2, 3, 6)),
            dma((2, 3, 6)),
            dma((2, 3, 6)),
            dma((2, NZ - 1)),
            dma((2, NZ - 1)),
            dma((2, 2 * NZ)),
            dma((2, 2 * NZ)),
            dma((5,)),
        ],
        name="clip_conv",
        compiler_params=pltpu.CompilerParams(
            collective_id=0, has_side_effects=True, vmem_limit_bytes=44 * 2**20
        ),
    )(*(pin(a, pltpu.HBM) for a in (lengths, clips[0], w_time, w_down, cotangent[0])))
    reduced, grad_clips, grad_time, grad_down = pl.pallas_call(
        deliver,
        out_shape=(
            jax.ShapeDtypeStruct((HD, S, C), BF),
            jax.ShapeDtypeStruct((FD, S, C), BF),
            jax.ShapeDtypeStruct((3, 32, C), F32),
            jax.ShapeDtypeStruct((3, 32, C), F32),
        ),
        in_specs=[vmem] * 3,
        out_specs=(hbm,) * 4,
        scratch_shapes=[
            pltpu.VMEM((3, 32, C), F32),
            pltpu.VMEM((3, 32, C), F32),
            dma((4,)),
        ],
        name="deliver",
        compiler_params=pltpu.CompilerParams(vmem_limit_bytes=16 * 2**20),
    )(reduced, grad_clips, pieces)
    return reduced[None], grad_clips[None], grad_time, grad_down


def deliver(reduced, grad_clips, pieces, reduced_out, clips_out, time_out, down_out, time, down, sem):
    pairs = ((grad_clips, clips_out), (reduced, reduced_out), (time, time_out), (down, down_out))
    stores = [pltpu.make_async_copy(a, b, sem.at[i]) for i, (a, b) in enumerate(pairs)]
    stores[0].start()
    stores[1].start()
    for g, full in ((0, time), (1, down)):
        for r in range(2):
            for q in range(4):
                for l in range(2):
                    full[:, l * 16 + r * 8 : l * 16 + r * 8 + 8, q * 128 : q * 128 + 128] = pieces[
                        g, r * 4 + q, l
                    ].astype(F32)
        stores[2 + g].start()
    for copy in stores:
        copy.wait()


def solution(mesh):
    in_specs = (
        P("group", "tm", None, None),
        P("group", None),
        P(None, "tm", None),
        P(None, "tm", None),
        P("group", "tm", None, None),
    )
    out_specs = (
        P("group", "tm", None, None),
        P("group", "tm", None, None),
        P(None, "tm", None),
        P(None, "tm", None),
    )
    return jax.shard_map(shards, mesh=mesh, in_specs=in_specs, out_specs=out_specs, check_vma=False)
```

```python
import functools

import jax
import jax.numpy as jnp
from jax import lax
from jax.experimental import pallas as pl
from jax.experimental.pallas import tpu as pltpu
from jax.sharding import PartitionSpec as P

MESH = pl.DeviceIdType.MESH
BF = jnp.bfloat16
F32 = jnp.float32
FD, HD, S, C, NC = 8, 4, 128, 512, 8
NT = 16
NZ = 8
EPS = 1e-06


def dot(a, b, ca, cb):
    return lax.dot_general(a, b, (((ca,), (cb,)), ((), ())), preferred_element_type=F32)


def device(x, y, z, core):
    return {"tm": y * 4 + (x // 2) * 2 + core, "group": z * 2 + x % 2}


def kernel(
    lengths_in,
    clips_in,
    wt_own,
    wd_own,
    cot_in,
    reduced,
    grad_clips,
    pieces,
    lengths,
    clips,
    wt,
    wd,
    clips_halo,
    cot_ext,
    h_ext,
    taps,
    gh,
    gm,
    hid,
    dtaps,
    gtap,
    stage,
    acc,
    core_out,
    core_in,
    outer_out,
    outer_in,
    inner_out,
    inner_in,
    z_wide,
    z_out,
    z_in,
    piece,
    w_send,
    w_recv,
    halo_send,
    halo_recv,
    core_send,
    core_recv,
    outer_send,
    outer_recv,
    inner_send,
    inner_recv,
    z_send,
    z_recv,
    p_send,
    p_recv,
    l_sem,
):
    t = lax.axis_index("tm")
    group = lax.axis_index("group")
    y, xh, c = t // 4, (t // 2) % 2, t % 2
    z, xl = group // 2, group % 2
    x = 2 * xh + xl

    def at(dx, dy, dz, dc):
        return device((x + dx + 4) % 4, (y + dy + 4) % 4, (z + dz + NZ) % NZ, (c + dc) % 2)

    sibling = at(0, 0, 0, 1)
    up, down = at(0, 1, 0, 0), at(0, -1, 0, 0)
    mirror = device(3 - x, y, z, c)
    step = 2 * c - 1
    far = {"tm": (t + step + NT) % NT, "group": group}

    def remote(src, dst, send, recv, target):
        return pltpu.make_async_remote_copy(
            src_ref=src,
            dst_ref=dst,
            send_sem=send,
            recv_sem=recv,
            device_id=target,
            device_id_type=MESH,
        )

    lengths_load = pltpu.make_async_copy(lengths_in, lengths, l_sem.at[4])
    lengths_load.start()

    barrier = pltpu.get_barrier_semaphore()
    peers = [sibling, far]
    peers += [at(d, 0, 0, 0) for d in range(1, 4)] + [at(0, d, 0, 0) for d in range(1, 4)]
    peers += [at(0, 0, d, 0) for d in range(1, NZ)]
    mate = 1 - 2 * xl
    peers += [at(mate, 0, d, 0) for d in range(1, NZ)]
    for peer in peers:
        pl.semaphore_signal(barrier, inc=1, device_id=peer, device_id_type=MESH)
    pl.semaphore_wait(barrier, len(peers))

    def clips_copy(f, target):
        return remote(
            clips_in.at[FD - 4 + f], clips_halo.at[f], halo_send.at[f], halo_recv.at[f], target
        )

    def cot_copy(f, target):
        return remote(
            cot_in.at[f], cot_ext.at[HD + f], halo_send.at[4 + f], halo_recv.at[4 + f], target
        )

    after = {"tm": (t + 1) % NT, "group": group}
    before = {"tm": (t + NT - 1) % NT, "group": group}

    mine = (z + xl) % 2

    def cut(full, owner, half, lane, width):
        row = pl.multiple_of(owner * 32 + half * 16, 16)
        return full.at[:, pl.ds(row, 16), pl.ds(lane, width)]

    def owner_of(dy, other):
        h = 1 - xh if other else xh
        return ((y + dy + 4) % 4) * 4 + h * 2 + c

    blocks = [(0, 1), (-1, 0), (1, 0), (2, 0), (-1, 1), (1, 1), (2, 1)]
    ahead, behind, beside = at(0, 0, 1, 0), at(0, 0, -1, 0), at(mate, 0, 0, 0)
    up2 = at(0, 2, 0, 0)

    def block_copy(w, number, slot, src, dst, to):
        return remote(src, dst, w_send.at[w, number], w_recv.at[w, slot], to)

    def half_copy(w, number, slot, owner, half, to, src=None):
        dst = cut((wd, wt)[w], owner, half, 0, C)
        return block_copy(w, number, slot, dst if src is None else src, dst, to)

    def tap_copy(w, number, slot, owner, half, tap, to):
        row = pl.multiple_of(owner * 32 + half * 16, 16)
        dst = (wd, wt)[w].at[tap, pl.ds(row, 16), :]
        return block_copy(w, number, slot, dst, dst, to)

    def whole(w, owner):
        return (wd, wt)[w].at[:, pl.ds(pl.multiple_of(owner * 32, 32), 32), :]

    def first_sends(w):
        own = (wd_own, wt_own)[w]
        half = own.at[:, pl.ds(pl.multiple_of(mine * 16, 16), 16), :]
        rest = own.at[:, pl.ds(pl.multiple_of(16 - mine * 16, 16), 16), :]
        return [
            half_copy(w, 0, 0, t, 1 - mine, mirror, rest),
            half_copy(w, 1, 1, t, mine, up, half),
            half_copy(w, 2, 2, t, mine, down, half),
            half_copy(w, 3, 3, t, mine, up2, half),
            block_copy(w, 4, 21, own, whole(w, t), sibling),
        ]

    def passes(w, index):
        owner = owner_of(*blocks[index])
        sends = []
        if index == 0:
            sends = [
                half_copy(w, 5, 4, owner, mine, up),
                half_copy(w, 6, 5, owner, mine, down),
                half_copy(w, 7, 6, owner, mine, up2),
            ]
        return sends + [
            tap_copy(w, 8 + index, 7 + index, owner, mine, 0, ahead),
            tap_copy(w, 15 + index, 14 + index, owner, mine, 2, behind),
            tap_copy(w, 36 + index, 36 + index, owner, mine, 1, beside),
            half_copy(w, 22 + index, 22 + index, owner, mine, sibling),
        ]

    def last_pass(w, index):
        owner = owner_of(*blocks[index])
        return half_copy(w, 29 + index, 29 + index, owner, 1 - mine, sibling)

    def own_copy(w):
        return pltpu.make_async_copy((wd_own, wt_own)[w], whole(w, t), l_sem.at[w])

    def arrive(w, *indices):
        for index in indices:
            owner = owner_of(*blocks[index])
            half_copy(w, 0, index, owner, mine, sibling).wait_recv()
            for copy in passes(w, index):
                copy.start()

    def arrive_z(w, *indices):
        for index in indices:
            owner = owner_of(*blocks[index])
            tap_copy(w, 0, 7 + index, owner, 1 - mine, 0, sibling).wait_recv()
            tap_copy(w, 0, 14 + index, owner, 1 - mine, 2, sibling).wait_recv()
            tap_copy(w, 0, 36 + index, owner, 1 - mine, 1, sibling).wait_recv()
            last_pass(w, index).start()

    def finish_weights(w):
        own_copy(w).wait()
        other = 1 - 2 * c
        block_copy(w, 0, 21, whole(w, t + other), whole(w, t + other), sibling).wait_recv()
        for index in range(7):
            owner = owner_of(*blocks[index]) + other
            half_copy(w, 0, 22 + index, owner, mine, sibling).wait_recv()
            half_copy(w, 0, 29 + index, owner, 1 - mine, sibling).wait_recv()

    clips_load = pltpu.make_async_copy(clips_in, clips, l_sem.at[2])
    cot_load = pltpu.make_async_copy(cot_in, cot_ext.at[pl.ds(0, HD)], l_sem.at[3])
    clips_load.start()
    cot_load.start()

    def send_cot(f):
        @pl.when(t > 0)
        def _():
            cot_copy(f, before).start()

    def send_clips(f):
        @pl.when(t < NT - 1)
        def _():
            clips_copy(f, after).start()

    for copy in first_sends(0):
        copy.start()
    send_cot(0)
    own_copy(0).start()
    own_copy(1).start()

    lengths_load.wait()

    def length(i):
        return lengths[0, i]

    ends = [length(0)]
    for i in range(1, NC):
        ends.append(ends[-1] + length(i))
    first = t * FD

    def opens(frame):
        f = first + frame
        hit = f == 0
        for end in ends:
            hit = jnp.logical_or(hit, f == end)
        return hit

    opening = {i: opens(i) for i in range(-3, 11)}

    def live(k, frame):
        if k == 0:
            return None
        out = jnp.logical_not(opening[frame])
        if k == 2:
            out = jnp.logical_and(out, jnp.logical_not(opening[frame - 1]))
        return out

    def masked(keep, value):
        return value if keep is None else jnp.where(keep, value, jnp.zeros_like(value))

    def features(block):
        wide = block.astype(F32)
        scale = lax.rsqrt(jnp.mean(wide * wide, axis=-1, keepdims=True) + EPS)
        v = wide * scale
        return (v / (1.0 + jnp.exp(-v))).astype(BF)

    def feature_body(i, _):
        h_ext[4 + i] = features(clips[i])
        return 0

    clips_load.wait()
    lax.fori_loop(0, 2, feature_body, 0)
    arrive(0, 0)
    send_cot(1)
    for copy in first_sends(1):
        copy.start()
    lax.fori_loop(2, 4, feature_body, 0)
    arrive(0, 1, 2, 3)
    send_clips(3)
    lax.fori_loop(4, 6, feature_body, 0)
    arrive(1, 0)
    arrive(0, 4, 5, 6)
    send_clips(2)
    lax.fori_loop(6, FD, feature_body, 0)
    arrive(1, 1, 2, 3)
    send_clips(1)
    send_clips(0)
    arrive_z(0, 0, 1, 2, 3, 4, 5, 6)
    cot_load.wait()

    @pl.when(t < NT - 1)
    def _():
        cot_copy(0, before).wait_recv()
        cot_copy(1, before).wait_recv()

    @pl.when(t == NT - 1)
    def _():
        cot_ext[pl.ds(HD, 2)] = jnp.zeros((2, S, C), BF)

    finish_weights(0)

    flat0 = cot_ext[pl.ds(0, 5)].reshape(5 * S, C)
    flat1 = cot_ext[pl.ds(1, 5)].reshape(5 * S, C)
    p0 = dot(flat0, wd[0], 1, 1).reshape(5, S, C)
    for j in range(5):
        gh[2 * j] = p0[j]
    arrive(1, 4, 5, 6)
    p2 = dot(flat1, wd[2], 1, 1).reshape(5, S, C)
    for j in range(5):
        total = gh[2 * j] + masked(live(2, 2 * j + 2), p2[j])
        gh[2 * j] = total
        gm[2 * j] = total.astype(BF)
    p1 = dot(flat1, wd[1], 1, 1).reshape(5, S, C)
    for j in range(5):
        total = masked(live(1, 2 * j + 2), p1[j])
        gh[2 * j + 1] = total
        gm[2 * j + 1] = total.astype(BF)

    arrive_z(1, 0, 1, 2, 3)

    def core_copy(g, k):
        return remote(
            core_out.at[g, k], core_in.at[g, k], core_send.at[g, k], core_recv.at[g, k], sibling
        )

    def contribute(g, k, value):
        stage[g] = value.reshape(4, 2, 2, 2, 16, C)
        for yy in range(4):
            for h in range(2):
                for l in range(2):
                    acc[g, k, 2 * h + l, yy] = stage[g, yy, h, c, l]
                    core_out[g, k, 2 * h + l, yy] = stage[g, yy, h, 1 - c, l].astype(BF)
        core_copy(g, k).start()

    def lanes(h):
        return pl.ds(h * (C // 2), C // 2)

    def line(h, d):
        return at(d, 0, 0, 0) if h == 0 else at(0, d, 0, 0)

    def outer_copy(g, k, h, d):
        i = 3 * h + d - 1
        return remote(
            outer_out.at[g, k, i],
            outer_in.at[g, k, i],
            outer_send.at[g, k, i],
            outer_recv.at[g, k, i],
            line(h, d),
        )

    def inner_copy(g, k, h, d):
        i = 3 * h + d - 1
        return remote(
            inner_out.at[g, k, i],
            inner_in.at[g, k, i],
            inner_send.at[g, k, i],
            inner_recv.at[g, k, i],
            line(1 - h, d),
        )

    order = [(h, d) for d in (2, 1, 3) for h in range(2)]

    def reduce_tap(g, k):
        core_copy(g, k).wait_recv()
        acc[g, k] = acc[g, k] + core_in[g, k].astype(F32)
        for h, d in order:
            if h == 0:
                block = acc[g, k, (x + d) % 4, :, :, lanes(h)]
            else:
                block = acc[g, k, :, (y + d) % 4, :, lanes(h)]
            outer_out[g, k, 3 * h + d - 1] = block.astype(BF)
            outer_copy(g, k, h, d).start()

    def inner_start(g, k):
        for h, d in order:
            outer_copy(g, k, h, d).wait_recv()
        for h in range(2):
            ref = acc.at[g, k, x] if h == 0 else acc.at[g, k, :, y]
            total = ref[:, :, lanes(h)]
            for d in range(1, 4):
                total = total + outer_in[g, k, 3 * h + d - 1].astype(F32)
            ref[:, :, lanes(h)] = total
        for h, d in order:
            if h == 0:
                block = acc[g, k, x, (y + d) % 4, :, lanes(h)]
            else:
                block = acc[g, k, (x + d) % 4, y, :, lanes(h)]
            inner_out[g, k, 3 * h + d - 1] = block.astype(BF)
            inner_copy(g, k, h, d).start()

    def z_copy(g, d):
        return remote(
            z_out.at[g, (z + d) % NZ],
            z_in.at[g, d - 1],
            z_send.at[g, d - 1],
            z_recv.at[g, d - 1],
            at(0, 0, d, 0),
        )

    def z_start(g):
        for k in range(3):
            for h, d in order:
                inner_copy(g, k, h, d).wait_recv()
            for h in range(2):
                total = acc[g, k, x, y, :, lanes(h)]
                for d in range(1, 4):
                    total = total + inner_in[g, k, 3 * h + d - 1].astype(F32)
                for r in range(2):
                    for q in range(2):
                        part = total[r * 8 : r * 8 + 8, q * 128 : q * 128 + 128]
                        z_wide[g, r * 4 + h * 2 + q, k] = part
                        z_out[g, r * 4 + h * 2 + q, k] = part.astype(BF)
        for d in (4, 3, 5, 2, 6, 1, 7):
            z_copy(g, d).start()

    def piece_copy(g, other, d):
        number = other * NZ + d - 1
        return remote(
            piece.at[g],
            pieces.at[g, z, xl],
            p_send.at[g, number],
            p_recv.at[g, number],
            at(mate * other, 0, d, 0),
        )

    sends = [(other, d) for d in (4, 3, 5, 2, 6, 1, 7) for other in (1, 0)] + [(1, 0)]

    def piece_start(g):
        total = z_wide[g, z]
        for d in range(1, NZ):
            z_copy(g, d).wait_recv()
            total = total + z_in[g, d - 1].astype(F32)
        piece[g] = total.astype(BF)
        for other, d in sends:
            piece_copy(g, other, d).start()
        pieces[g, z, xl] = piece[g]

    def time_grad(k):
        left = h_ext[pl.ds(4, FD)] if k == 0 else taps[k, pl.ds(2, FD)]
        left = left.reshape(FD * S, C)
        contribute(0, k, dot(left, gm[pl.ds(0, FD)].reshape(FD * S, C), 0, 0))

    time_grad(0)
    arrive_z(1, 4, 5, 6)

    @pl.when(t > 0)
    def _():
        for f in range(4):
            clips_copy(f, after).wait_recv()

    @pl.when(t == 0)
    def _():
        clips_halo[...] = jnp.zeros((4, S, C), BF)

    def halo_body(i, _):
        h_ext[i] = features(clips_halo[i])
        return 0

    lax.fori_loop(0, 4, halo_body, 0)
    for k in range(3):
        for i in range(10):
            taps[k, i] = masked(live(k, i - 2), h_ext[i + 2 - k])

    time_grad(1)
    reduce_tap(0, 0)
    time_grad(2)
    reduce_tap(0, 1)
    for k in range(1, 3):
        for f in range(FD):
            gtap[k - 1, f] = masked(live(k, f + k), gm[f + k])
    reduce_tap(0, 2)
    finish_weights(1)

    def hidden_three(i, wide):
        total = wide.astype(F32).reshape(3 * S, C)
        for k in range(3):
            total = total + dot(taps[k, pl.ds(i, 3)].reshape(3 * S, C), wt[k], 1, 0)
        hid[pl.ds(i, 3)] = total.astype(BF).reshape(3, S, C)

    hidden_three(0, jnp.concatenate([clips_halo[pl.ds(2, 2)], clips[pl.ds(0, 1)]], axis=0))
    hidden_three(3, clips[pl.ds(1, 3)])
    hidden_three(6, clips[pl.ds(4, 3)])
    for k in range(3):
        for j in range(HD):
            dtaps[k, j] = masked(live(k, 2 * j), hid[2 * j + 2 - k])

    def down_grad(k):
        contribute(1, k, dot(dtaps[k].reshape(HD * S, C), cot_ext[pl.ds(0, HD)].reshape(HD * S, C), 0, 0))

    down_grad(0)
    down_grad(1)
    down_grad(2)
    reduce_tap(1, 0)
    reduce_tap(1, 1)
    inner_start(0, 0)
    reduce_tap(1, 2)
    inner_start(0, 1)
    inner_start(0, 2)
    total = dot(dtaps[0].reshape(HD * S, C), wd[0], 1, 0)
    total = total + dot(dtaps[1].reshape(HD * S, C), wd[1], 1, 0)
    total = total + dot(dtaps[2].reshape(HD * S, C), wd[2], 1, 0)
    reduced[...] = total.astype(BF).reshape(HD, S, C)

    def clips_pair(i, _):
        here = pl.ds(2 * i, 2)
        g = dot(gm[here].reshape(2 * S, C), wt[0], 1, 1)
        g = g + dot(gtap[0, here].reshape(2 * S, C), wt[1], 1, 1)
        g = g + dot(gtap[1, here].reshape(2 * S, C), wt[2], 1, 1)
        wide = clips[here].astype(F32).reshape(2 * S, C)
        scale = lax.rsqrt(jnp.mean(wide * wide, axis=-1, keepdims=True) + EPS)
        v = wide * scale
        sig = 1.0 / (1.0 + jnp.exp(-v))
        d = g * (sig * (1.0 + v * (1.0 - sig)))
        inner = jnp.mean(d * v, axis=-1, keepdims=True)
        grad = (d - v * inner) * scale
        grad_clips[here] = (gh[here].reshape(2 * S, C) + grad).astype(BF).reshape(2, S, C)
        return 0

    z_start(0)
    inner_start(1, 0)
    inner_start(1, 1)
    inner_start(1, 2)
    lax.fori_loop(0, 1, clips_pair, 0)
    z_start(1)
    piece_start(0)
    lax.fori_loop(1, 2, clips_pair, 0)
    piece_start(1)
    lax.fori_loop(2, 4, clips_pair, 0)
    for g in range(2):
        for other, d in sends:
            piece_copy(g, other, d).wait()

    @pl.when(t > 0)
    def _():
        cot_copy(0, before).wait_send()
        cot_copy(1, before).wait_send()

    @pl.when(t < NT - 1)
    def _():
        for f in range(4):
            clips_copy(f, after).wait_send()

    for w in range(2):
        for copy in first_sends(w):
            copy.wait_send()
        for index in range(7):
            for copy in passes(w, index):
                copy.wait_send()
            last_pass(w, index).wait_send()
    for g in range(2):
        for k in range(3):
            core_copy(g, k).wait_send()
        for h, d in order:
            for k in range(3):
                outer_copy(g, k, h, d).wait_send()
                inner_copy(g, k, h, d).wait_send()
        for d in range(1, NZ):
            z_copy(g, d).wait_send()


def shards(clips, lengths, w_time, w_down, cotangent):
    vmem = pl.BlockSpec(memory_space=pltpu.VMEM)
    hbm = pl.BlockSpec(memory_space=pltpu.HBM)
    pin = pltpu.with_memory_space_constraint
    dma = pltpu.SemaphoreType.DMA
    reduced, grad_clips, pieces = pl.pallas_call(
        kernel,
        out_shape=(
            jax.ShapeDtypeStruct((HD, S, C), BF),
            jax.ShapeDtypeStruct((FD, S, C), BF),
            jax.ShapeDtypeStruct((2, NZ, 2, 3, 8, 128), BF),
        ),
        in_specs=[hbm] * 5,
        out_specs=(vmem, vmem, vmem),
        scratch_shapes=[
            pltpu.SMEM((1, NC), jnp.int32),
            pltpu.VMEM((FD, S, C), BF),
            pltpu.VMEM((3, C, C), BF),
            pltpu.VMEM((3, C, C), BF),
            pltpu.VMEM((4, S, C), BF),
            pltpu.VMEM((HD + 2, S, C), BF),
            pltpu.VMEM((FD + 4, S, C), BF),
            pltpu.VMEM((3, FD + 2, S, C), BF),
            pltpu.VMEM((FD + 2, S, C), F32),
            pltpu.VMEM((FD + 2, S, C), BF),
            pltpu.VMEM((FD + 1, S, C), BF),
            pltpu.VMEM((3, HD, S, C), BF),
            pltpu.VMEM((2, FD, S, C), BF),
            pltpu.VMEM((2, 4, 2, 2, 2, 16, C), F32),
            pltpu.VMEM((2, 3, 4, 4, 16, C), F32),
            pltpu.VMEM((2, 3, 4, 4, 16, C), BF),
            pltpu.VMEM((2, 3, 4, 4, 16, C), BF),
            pltpu.VMEM((2, 3, 6, 4, 16, C // 2), BF),
            pltpu.VMEM((2, 3, 6, 4, 16, C // 2), BF),
            pltpu.VMEM((2, 3, 6, 16, C // 2), BF),
            pltpu.VMEM((2, 3, 6, 16, C // 2), BF),
            pltpu.VMEM((2, NZ, 3, 8, 128), F32),
            pltpu.VMEM((2, NZ, 3, 8, 128), BF),
            pltpu.VMEM((2, NZ - 1, 3, 8, 128), BF),
            pltpu.VMEM((2, 3, 8, 128), BF),
            dma((2, 43)),
            dma((2, 43)),
            dma((6,)),
            dma((6,)),
            dma((2, 3)),
            dma((2, 3)),
            dma((2, 3, 6)),
            dma((2, 3, 6)),
            dma((2, 3, 6)),
            dma((2, 3, 6)),
            dma((2, NZ - 1)),
            dma((2, NZ - 1)),
            dma((2, 2 * NZ)),
            dma((2, 2 * NZ)),
            dma((5,)),
        ],
        name="clip_conv",
        compiler_params=pltpu.CompilerParams(
            collective_id=0, has_side_effects=True, vmem_limit_bytes=44 * 2**20
        ),
    )(*(pin(a, pltpu.HBM) for a in (lengths, clips[0], w_time, w_down, cotangent[0])))
    reduced, grad_clips, grad_time, grad_down = pl.pallas_call(
        deliver,
        out_shape=(
            jax.ShapeDtypeStruct((HD, S, C), BF),
            jax.ShapeDtypeStruct((FD, S, C), BF),
            jax.ShapeDtypeStruct((3, 32, C), F32),
            jax.ShapeDtypeStruct((3, 32, C), F32),
        ),
        in_specs=[vmem] * 3,
        out_specs=(hbm,) * 4,
        scratch_shapes=[
            pltpu.VMEM((3, 32, C), F32),
            pltpu.VMEM((3, 32, C), F32),
            dma((4,)),
        ],
        name="deliver",
        compiler_params=pltpu.CompilerParams(vmem_limit_bytes=16 * 2**20),
    )(reduced, grad_clips, pieces)
    return reduced[None], grad_clips[None], grad_time, grad_down


def deliver(reduced, grad_clips, pieces, reduced_out, clips_out, time_out, down_out, time, down, sem):
    pairs = ((grad_clips, clips_out), (reduced, reduced_out), (time, time_out), (down, down_out))
    stores = [pltpu.make_async_copy(a, b, sem.at[i]) for i, (a, b) in enumerate(pairs)]
    stores[0].start()
    stores[1].start()
    for g, full in ((0, time), (1, down)):
        for r in range(2):
            for q in range(4):
                for l in range(2):
                    full[:, l * 16 + r * 8 : l * 16 + r * 8 + 8, q * 128 : q * 128 + 128] = pieces[
                        g, r * 4 + q, l
                    ].astype(F32)
        stores[2 + g].start()
    for copy in stores:
        copy.wait()


def solution(mesh):
    in_specs = (
        P("group", "tm", None, None),
        P("group", None),
        P(None, "tm", None),
        P(None, "tm", None),
        P("group", "tm", None, None),
    )
    out_specs = (
        P("group", "tm", None, None),
        P("group", "tm", None, None),
        P(None, "tm", None),
        P(None, "tm", None),
    )
    return jax.shard_map(shards, mesh=mesh, in_specs=in_specs, out_specs=out_specs, check_vma=False)
```
